256 devices in a mesh: upd: 8 (over x, core), col: 32 (over z, y).
Axes of the slice: x: 4, y: 4, z: 8, core: 2. Of those that a mesh axis runs over, the one named last changes fastest.
Arguments:
- panel: bfloat16 [32, 8, 1024, 1024], P('col', None, 'upd'), may hold values from -6 to 6
- diag_tiles: bfloat16 [32, 1024, 1024], P('col', 'upd'), may hold values from -6 to 6
- dinv: bfloat16 [32, 1024, 1024], P('col'), may hold values from -1 to 1, as said below
- u_fac: bfloat16 [32, 8, 8, 96, 1024], P('col', None, 'upd'), may hold values from -1.1953125 to 1.1953125
- v_fac: bfloat16 [32, 8, 8, 96, 1024], P('col', None, 'upd'), may hold values from -1.1953125 to 1.1953125
- ranks: int32 [32, 8, 8], P('col', None, 'upd'), may hold values from 1 to 96, as said below
- sketch: bfloat16 [32, 64, 1024], P('col'), may hold values from -6 to 6
Outputs:
- panel_out: bfloat16 [32, 8, 1024, 1024], P('col', None, 'upd')
- diag_out: float32 [32, 1024, 1024], P('col', 'upd')
The draws below stay inside these ranges and needn't reach their ends.
Inputs may be any that keep to these rules, and one draw needn't show every extreme that they name: `ranks`: in every panel tile at least two of the 8 pieces have rank 96. `dinv`: each block is lower triangular with a positive diagonal.
All inputs are finite; a program needn't handle non-finite values.
Results may differ from the reference program's by a relative error of at most 0.014.
Values may be sent and summed in bfloat16 or wider, within the bound.
No kernel may reach another device: no remote copies, remote signals or barrier semaphores. Data moves between devices by JAX's collectives and lax.ppermute only.
A program may use at most 64 MiB of HBM per device.

```python
import math
import jax
import jax.numpy as jnp
from jax import lax

B = 1024
RK = 64
MAXR = 96
BAND = 8
NCOL = 32
NUPD = 8


def draw_ranks(key, part):
    base = jax.random.fold_in(key, 11)
    key_a, key_b, key_c = jax.random.split(base, 3)
    shape = (NCOL, BAND, NUPD)
    scores = jax.random.randint(key_a, shape, 0, 1048576) * NUPD + jnp.arange(NUPD, dtype=jnp.int32)
    order = jnp.argsort(jnp.argsort(scores, axis=-1), axis=-1)
    first = jax.random.randint(key_b, shape, 0, MAXR)
    second = jax.random.randint(key_c, shape, 0, MAXR)
    rest = 1 + first * second // MAXR
    return jnp.where(order < 2, MAXR, rest).astype(jnp.int32)


def draw_dinv(key, part):
    base = jax.random.fold_in(key, 23)
    key_a, key_b = jax.random.split(base, 2)
    logd = jax.random.uniform(key_a, (NCOL, B), jnp.float32, math.log(0.5), math.log(2.0))
    diagonal = 0.075 * jnp.exp(logd)
    lower = jax.random.normal(key_b, (NCOL, B, B), jnp.float32) * (0.1 / math.sqrt(B))
    rows = jnp.arange(B, dtype=jnp.int32)[:, None]
    cols = jnp.arange(B, dtype=jnp.int32)[None, :]
    result = jnp.where(cols < rows, lower, 0.0) + jnp.where(cols == rows, diagonal[:, :, None], 0.0)
    return result.astype(jnp.bfloat16)


def shard_levels(own_key, shape, cuts, smallest, high):
    def one(axis_at, parts):
        steps = jax.random.uniform(jax.random.fold_in(jax.random.fold_in(own_key, 6), axis_at), (parts,), jnp.float32, smallest / len(cuts), high / len(cuts))
        return jnp.repeat(jnp.exp(steps), shape[axis_at] // parts).reshape((-1,) + (1,) * (len(shape) - axis_at - 1))

    loudness = one(*cuts[0])
    for cut in cuts[1:]:
        loudness = loudness * one(*cut)
    return loudness


def noise(stream_key, shape, scale, bound, shards=(), kind=jnp.bfloat16):
    drawn = scale * jax.random.normal(stream_key, shape, jnp.float32)
    if shards:
        drawn = drawn * shard_levels(stream_key, shape, shards, -0.22, 0.18)
    return jnp.clip(drawn, -bound, bound).astype(kind)


def setup_inputs(seed: int = 0) -> dict:
    streams_of = jax.random.split(jax.random.key(seed), 8)
    panel = noise(streams_of[0], (NCOL, BAND, B, B), 1.0, 6.0, ((0, 32), (2, 8)))
    diag_tiles = noise(streams_of[1], (NCOL, B, B), 1.0, 6.0, ((0, 32), (1, 8)))
    dinv = draw_dinv(jax.random.fold_in(streams_of[7], 71), 0)
    u_fac = noise(streams_of[3], (NCOL, BAND, NUPD, MAXR, B), 0.2, 1.1953125, ((0, 32), (2, 8)))
    v_fac = noise(streams_of[4], (NCOL, BAND, NUPD, MAXR, B), 0.2, 1.1953125, ((0, 32), (2, 8)))
    ranks = draw_ranks(jax.random.fold_in(streams_of[7], 71), 0)
    sketch = noise(streams_of[6], (NCOL, RK, B), 1.0, 6.0, ((0, 32),))
    return {"panel": panel, "diag_tiles": diag_tiles, "dinv": dinv, "u_fac": u_fac, "v_fac": v_fac, "ranks": ranks, "sketch": sketch}


def orthonormal(summed):
    gram = jnp.einsum('kb,lb->kl', summed, summed, precision=lax.Precision.HIGHEST)
    chol = jnp.linalg.cholesky(gram)
    return jax.scipy.linalg.solve_triangular(chol, summed, lower=True).astype(jnp.bfloat16)

def tile_factor(tile, left_factor, right_factor, piece_ranks, sketch_col, dinv_col):
    slots = jnp.arange(MAXR, dtype=jnp.int32)
    keep = slots[None, :, None] < piece_ranks[:, None, None]
    random_probe = jnp.einsum('urb,kb->urk', right_factor.astype(jnp.float32), sketch_col.astype(jnp.float32))
    random_probe = jnp.where(keep, random_probe, 0.0).astype(jnp.bfloat16)
    summed = jnp.einsum('urb,urk->kb', left_factor.astype(jnp.float32), random_probe.astype(jnp.float32))
    range_basis = orthonormal(summed)
    coefficient_matrix = jnp.einsum('urb,kb->urk', left_factor.astype(jnp.float32), range_basis.astype(jnp.float32))
    coefficient_matrix = jnp.where(keep, coefficient_matrix, 0.0).astype(jnp.bfloat16)
    cross_term = jnp.einsum('urb,urk->kb', right_factor.astype(jnp.float32), coefficient_matrix.astype(jnp.float32)).astype(jnp.bfloat16)
    approximation = jnp.dot(range_basis.T.astype(jnp.float32), cross_term.astype(jnp.float32), preferred_element_type=jnp.float32)
    updated_tile = (tile.astype(jnp.float32) - approximation).astype(jnp.bfloat16)
    return jnp.dot(updated_tile.astype(jnp.float32), dinv_col.T.astype(jnp.float32), preferred_element_type=jnp.float32).astype(jnp.bfloat16)

def column_factor(pack):
    tiles, dinv_col, left_factor, right_factor, col_ranks, sketch_col = pack
    solve = lambda tile, lf, rf, rk: tile_factor(tile, lf, rf, rk, sketch_col, dinv_col)
    return jax.vmap(solve)(tiles, left_factor, right_factor, col_ranks)

def reference(panel, diag_tiles, dinv, u_fac, v_fac, ranks, sketch):
    factors = lax.map(column_factor, (panel, dinv, u_fac, v_fac, ranks, sketch))
    accum = diag_tiles.astype(jnp.float32)
    for shift_by in range(1, BAND + 1):
        if shift_by < NCOL:
            moved = factors[:NCOL - shift_by, shift_by - 1].astype(jnp.float32)
            accum = accum.at[shift_by:].add(-jnp.einsum('jrb,jnb->jrn', moved, moved))
    return (factors, accum)
```

```python
import jax
import jax.numpy as jnp
from jax import lax
from jax.experimental import pallas as pl
from jax.experimental.pallas import tpu as pltpu
from jax.sharding import PartitionSpec as P

F32 = jnp.float32
BF16 = jnp.bfloat16
AXES = ("upd", "col")
NU = 8
NX = 4
NC = 32
HALF = 5
BLK = 128


def dot(a, b, dims, precision=None):
    return lax.dot_general(a, b, (dims, ((), ())), precision=precision, preferred_element_type=F32)


def perm(block, route):
    pairs = []
    for u in range(NU):
        for c in range(NC):
            to = route(u, c)
            if to is not None:
                pairs.append((u * NC + c, to[0] * NC + to[1]))
    return lax.ppermute(block, AXES, pairs)


def along_x(k):
    return lambda u, c: ((u + 2 * k) % NU, c)


def along_upd(k):
    return lambda u, c: ((u + k) % NU, c)


def partner(u, c):
    return (u ^ 1, c)


def to_owner(k):
    def route(u, c):
        j = c + u + 1
        return None if j >= NC else ((u + k) % NU, j)

    return route


def sketch_kernel(where, ranks, v_ref, u_ref, sketch_ref, send_ref, keep_ref):
    k = pl.program_id(0)
    core = where[1]
    pair = (where[0] + k) % NX
    for side in range(2):
        which = core if side else 1 - core
        probe = dot(v_ref[which], sketch_ref[...], ((1,), (1,)))
        slots = lax.broadcasted_iota(jnp.int32, probe.shape, 0)
        probe = jnp.where(slots < ranks[2 * pair + which], probe, 0.0).astype(BF16)
        out = dot(probe, u_ref[which], ((0,), (0,)))
        if side:
            keep_ref[0] = out
        else:
            send_ref[0] = out.astype(BF16)


def sketch_call(where, ranks, v, u, sketch):
    tiles, slots, width = v.shape
    rk = sketch.shape[0]
    pairs = pl.BlockSpec((2, slots, width), lambda k, w, r: ((w[0] + k) % NX, 0, 0))
    return pl.pallas_call(
        sketch_kernel,
        out_shape=(
            jax.ShapeDtypeStruct((NX, rk, width), BF16),
            jax.ShapeDtypeStruct((NX, rk, width), F32),
        ),
        grid_spec=pltpu.PrefetchScalarGridSpec(
            num_scalar_prefetch=2,
            grid=(NX,),
            in_specs=[pairs, pairs, pl.BlockSpec((rk, width), lambda k, w, r: (0, 0))],
            out_specs=[
                pl.BlockSpec((1, rk, width), lambda k, w, r: (k, 0, 0)),
                pl.BlockSpec((1, rk, width), lambda k, w, r: (k, 0, 0)),
            ],
        ),
        name="sketch_product",
    )(where, ranks, v, u, sketch)


def project_kernel(where, ranks, u_ref, v_ref, *refs):
    bases, (send_ref, keep_ref) = refs[:NU], refs[NU:]
    d = pl.program_id(0)
    core = where[1]
    pair = (where[0] + NX - d) % NX
    for step in range(NX):

        @pl.when(d == step)
        def _(step=step):
            for side in range(2):
                which = core if side else 1 - core
                basis = bases[step if side else NX + step][...]
                coeff = dot(u_ref[which], basis, ((1,), (1,)))
                slots = lax.broadcasted_iota(jnp.int32, coeff.shape, 0)
                coeff = jnp.where(slots < ranks[2 * pair + which], coeff, 0.0).astype(BF16)
                out = dot(coeff, v_ref[which], ((0,), (0,)))
                if side:
                    keep_ref[0] = out
                else:
                    send_ref[0] = out.astype(BF16)


def project_call(where, ranks, u, v, bases):
    tiles, slots, width = v.shape
    rk = bases[0].shape[0]
    pairs = pl.BlockSpec((2, slots, width), lambda d, w, r: ((w[0] + NX - d) % NX, 0, 0))
    whole = pl.BlockSpec((rk, width), lambda d, w, r: (0, 0))
    out = pl.BlockSpec((1, rk, width), lambda d, w, r: ((NX - d) % NX, 0, 0))
    return pl.pallas_call(
        project_kernel,
        out_shape=(
            jax.ShapeDtypeStruct((NX, rk, width), BF16),
            jax.ShapeDtypeStruct((NX, rk, width), F32),
        ),
        grid_spec=pltpu.PrefetchScalarGridSpec(
            num_scalar_prefetch=2,
            grid=(NX,),
            in_specs=[pairs, pairs] + [whole] * NU,
            out_specs=[out, out],
        ),
        name="basis_product",
    )(where, ranks, u, v, *bases)


def pair_sum_kernel(keep_ref, got_ref, own_ref, a_ref, b_ref, c_ref):
    for k, ref in enumerate((own_ref, a_ref, b_ref, c_ref)):
        ref[...] = (keep_ref[k] + got_ref[k].astype(F32)).astype(ref.dtype)


def pair_sum(keep, got):
    shape = keep.shape[1:]
    return pl.pallas_call(
        pair_sum_kernel,
        out_shape=(jax.ShapeDtypeStruct(shape, F32),)
        + tuple(jax.ShapeDtypeStruct(shape, BF16) for _ in range(3)),
        name="pair_sum",
    )(keep, got)


def owner_parts(send, keep):
    got = perm(send, partner)
    own, *others = pair_sum(keep, got)
    return [own] + [perm(part, along_x(k + 1)) for k, part in enumerate(others)]


def basis_kernel(own_ref, a_ref, b_ref, c_ref, basis_ref):
    summed = own_ref[...] + a_ref[...].astype(F32) + b_ref[...].astype(F32) + c_ref[...].astype(F32)
    rk = summed.shape[0]
    gram = dot(summed, summed, ((1,), (1,)), lax.Precision.HIGHEST)
    rows = lax.broadcasted_iota(jnp.int32, (rk, rk), 0)
    cols = lax.broadcasted_iota(jnp.int32, (rk, rk), 1)
    row_at = lax.broadcasted_iota(jnp.int32, (rk, 1), 0)
    work = jnp.concatenate([gram, jnp.where(rows == cols, 1.0, 0.0)], axis=1)
    for k in range(rk):
        row = work[k : k + 1, :]
        scaled = row * (1.0 / work[k : k + 1, k : k + 1])
        col = jnp.where(row_at > k, work[:, k : k + 1], 0.0)
        work = work - col * scaled
    pivots = jnp.sum(jnp.where(rows == cols, work[:, :rk], 0.0), axis=1, keepdims=True)
    inverse = work[:, rk:] * lax.rsqrt(pivots)
    basis_ref[...] = dot(inverse, summed, ((1,), (0,)), lax.Precision.HIGHEST).astype(BF16)


def basis_call(parts):
    return pl.pallas_call(
        basis_kernel, out_shape=jax.ShapeDtypeStruct(parts[0].shape, BF16), name="orthonormal"
    )(*parts)


def gathered(own):
    mine = [own] + [perm(own, along_x(d)) for d in range(1, NX)]
    return mine + [perm(block, partner) for block in mine]


def split_kernel(where, panel_ref, *refs):
    outs, sems = refs[:-1], refs[-1]
    copies = []
    for k, out in enumerate(outs):
        copies.append(
            pltpu.make_async_copy(panel_ref.at[(where[2] + k) % NU], out, sems.at[k])
        )
    for copy in copies:
        copy.start()
    for copy in copies:
        copy.wait()


def split_panel(where, panel):
    shape = panel.shape[1:]
    anywhere = pl.BlockSpec(memory_space=pl.ANY)
    return pl.pallas_call(
        split_kernel,
        out_shape=tuple(jax.ShapeDtypeStruct(shape, BF16) for _ in range(NU)),
        in_specs=[pl.BlockSpec(memory_space=pltpu.SMEM), anywhere],
        out_specs=[anywhere] * NU,
        scratch_shapes=[pltpu.SemaphoreType.DMA((NU,))],
        name="split_panel",
    )(where, panel)


def tile_kernel(where, basis_ref, own_ref, a_ref, b_ref, c_ref, dinv_ref, *refs):
    rows = refs[:NU]
    cross_ref, outs, solved = refs[NU], refs[NU + 1 : NU + 1 + NU], refs[-1]
    cross = own_ref[...] + a_ref[...].astype(F32) + b_ref[...].astype(F32) + c_ref[...].astype(F32)
    cross = cross.astype(BF16)
    cross_ref[...] = cross
    dinv = dinv_ref[...]
    for k in range(NU):
        at = pl.multiple_of(((where[2] + NU - k) % NU) * BLK, BLK)
        part = basis_ref[:, pl.ds(at, BLK)]
        updated = (rows[k][...].astype(F32) - dot(part, cross, ((0,), (0,)))).astype(BF16)
        solved[k * BLK : (k + 1) * BLK] = dot(updated, dinv, ((1,), (1,))).astype(BF16)
    for k in range(HALF - 1):
        solved[(NU + k) * BLK : (NU + k + 1) * BLK] = solved[k * BLK : (k + 1) * BLK]
    for s in range(NU):
        k = (NU - s) % NU
        outs[s][...] = dot(
            solved[k * BLK : (k + 1) * BLK], solved[k * BLK : (k + HALF) * BLK], ((1,), (1,))
        ).astype(BF16)


def tile_call(where, basis, parts, dinv, rows):
    rk, width = basis.shape
    vmem = pl.BlockSpec(memory_space=pltpu.VMEM)
    return pl.pallas_call(
        tile_kernel,
        out_shape=(jax.ShapeDtypeStruct((rk, width), BF16),)
        + tuple(jax.ShapeDtypeStruct((BLK, HALF * BLK), BF16) for _ in range(NU)),
        in_specs=[pl.BlockSpec(memory_space=pltpu.SMEM)] + [vmem] * (6 + NU),
        out_specs=[vmem] * (1 + NU),
        scratch_shapes=[pltpu.VMEM(((NU + HALF - 1) * BLK, width), BF16)],
        name="tile_product",
    )(where, basis, *parts, dinv, *rows)


def rows_kernel(where, panel_ref, dinv_ref, *refs):
    bases, crosses, out_ref = refs[:NU], refs[NU : 2 * NU], refs[-1]
    d = pl.program_id(0)
    core = where[1]
    at = pl.multiple_of(where[2] * BLK, BLK)
    for step in range(NX):

        @pl.when(d == step)
        def _(step=step):
            for side in range(2):
                which = core if side else 1 - core
                source = step if side else NX + step
                part = bases[source][:, pl.ds(at, BLK)]
                lowrank = dot(part, crosses[source][...], ((0,), (0,)))
                updated = (panel_ref[which].astype(F32) - lowrank).astype(BF16)
                out_ref[which] = dot(updated, dinv_ref[...], ((1,), (1,))).astype(BF16)


def rows_call(where, panel, dinv, bases, crosses):
    rk, width = bases[0].shape
    pairs = pl.BlockSpec((2,) + panel.shape[1:], lambda d, w: ((w[0] + NX - d) % NX, 0, 0))
    whole = pl.BlockSpec((rk, width), lambda d, w: (0, 0))
    return pl.pallas_call(
        rows_kernel,
        out_shape=jax.ShapeDtypeStruct(panel.shape, BF16),
        grid_spec=pltpu.PrefetchScalarGridSpec(
            num_scalar_prefetch=1,
            grid=(NX,),
            in_specs=[pairs, pl.BlockSpec(dinv.shape, lambda d, w: (0, 0))] + [whole] * (2 * NU),
            out_specs=pairs,
        ),
        name="panel_rows",
    )(where, panel, dinv, *bases, *crosses)


def collect_kernel(*refs):
    got, (total_ref, a_ref, b_ref, c_ref) = refs[:NU], refs[NU:]
    total = got[0][...].astype(F32)
    for block in got[1:]:
        total = total + block[...].astype(F32)
    total_ref[...] = total
    for d, ref in ((1, a_ref), (2, b_ref), (3, c_ref)):
        ref[...] = total[:, d * BLK : (d + 1) * BLK].T


def collect_call(got):
    mirrored = jax.ShapeDtypeStruct((BLK, BLK), F32)
    return pl.pallas_call(
        collect_kernel,
        out_shape=(jax.ShapeDtypeStruct(got[0].shape, F32), mirrored, mirrored, mirrored),
        name="collect",
    )(*got)


def diag_kernel(where, diag_ref, total_ref, a_ref, b_ref, c_ref, out_ref):
    for d in range(HALF):
        at = pl.ds(pl.multiple_of(((where[2] + NU - d) % NU) * BLK, BLK), BLK)
        out_ref[:, at] = diag_ref[:, at].astype(F32) - total_ref[:, d * BLK : (d + 1) * BLK]
    for d, ref in ((1, a_ref), (2, b_ref), (3, c_ref)):
        at = pl.ds(pl.multiple_of(((where[2] + d) % NU) * BLK, BLK), BLK)
        out_ref[:, at] = diag_ref[:, at].astype(F32) - ref[...]


def diag_call(where, diag, total, mirrored):
    vmem = pl.BlockSpec(memory_space=pltpu.VMEM)
    return pl.pallas_call(
        diag_kernel,
        out_shape=jax.ShapeDtypeStruct(diag.shape, F32),
        in_specs=[pl.BlockSpec(memory_space=pltpu.SMEM)] + [vmem] * 5,
        out_specs=vmem,
        name="diagonal",
    )(where, diag, total, *mirrored)


def local(panel, diag_tiles, dinv, u_fac, v_fac, ranks, sketch):
    at = lax.axis_index("upd").astype(jnp.int32)
    where = jnp.stack([at // 2, at % 2, at])
    u, v, ranks = u_fac[0, :, 0], v_fac[0, :, 0], ranks[0, :, 0]

    parts = owner_parts(*sketch_call(where, ranks, v, u, sketch[0]))
    blocks = split_panel(where, panel[0])
    rows = [blocks[0]] + [perm(blocks[k], along_upd(k)) for k in range(1, NU)]
    basis = basis_call(parts)
    bases = gathered(basis)
    parts = owner_parts(*project_call(where, ranks, u, v, bases))
    cross, *products = tile_call(where, basis, parts, dinv[0], rows)
    got = [perm(block, to_owner(k)) for k, block in enumerate(products)]
    crosses = gathered(cross)
    panel_out = rows_call(where, panel[0], dinv[0], bases, crosses)
    total, *mirrored = collect_call(got)
    mirrored = [perm(block, along_upd(-d - 1)) for d, block in enumerate(mirrored)]
    diag_out = diag_call(where, diag_tiles[0], total, mirrored)
    return (panel_out[None], diag_out[None])


def solution(mesh):
    in_specs = (
        P("col", None, "upd", None),
        P("col", "upd", None),
        P("col", None, None),
        P("col", None, "upd", None, None),
        P("col", None, "upd", None, None),
        P("col", None, "upd"),
        P("col", None, None),
    )
    out_specs = (P("col", None, "upd", None), P("col", "upd", None))
    return jax.shard_map(local, mesh=mesh, in_specs=in_specs, out_specs=out_specs, check_vma=False)
```

```python
import jax
import jax.numpy as jnp
from jax import lax
from jax.experimental import pallas as pl
from jax.experimental.pallas import tpu as pltpu
from jax.sharding import PartitionSpec as P

F32 = jnp.float32
BF16 = jnp.bfloat16
AXES = ("upd", "col")
NU = 8
NX = 4
NC = 32
HALF = 5
BLK = 128
NEAR = ((1,), (1,))
LEFT = ((0,), (0,))
EXACT = lax.Precision.HIGHEST


def dot(a, b, dims, precision=None):
    return lax.dot_general(a, b, (dims, ((), ())), precision=precision, preferred_element_type=F32)


def place():
    at = lax.axis_index("upd")
    return at >> 1, at & 1


def perm(block, route):
    pairs = []
    for u in range(NU):
        for c in range(NC):
            to = route(u, c)
            if to is not None:
                pairs.append((u * NC + c, to[0] * NC + to[1]))
    return lax.ppermute(block, AXES, pairs)


def along_x(k):
    return lambda u, c: ((u + 2 * k) % NU, c)


def along_upd(k):
    return lambda u, c: ((u + k) % NU, c)


def partner(u, c):
    return (u ^ 1, c)


def to_column(k):
    def route(u, c):
        j = c + u // 2 + 1
        return None if j >= NC else ((u + 2 * k) % NU, j)

    return route


def four_on(u, c):
    return None if c + 4 >= NC else (u, c + 4)


def call(kernel, name, outs, ins, scalars=(), scratch=(), in_hbm=False):
    vmem = pl.BlockSpec(memory_space=pltpu.VMEM)
    if in_hbm:
        shapes = [jax.ShapeDtypeStruct(*out) for out in outs]
    else:
        shapes = [pltpu.VMEM(*out) for out in outs]
    out_spec = pl.BlockSpec(memory_space=pl.ANY) if in_hbm else vmem
    return pl.pallas_call(
        kernel,
        out_shape=shapes,
        in_specs=[pl.BlockSpec(memory_space=pltpu.SMEM)] * len(scalars) + [vmem] * len(ins),
        out_specs=[out_spec] * len(outs),
        scratch_shapes=list(scratch),
        compiler_params=pltpu.CompilerParams(vmem_limit_bytes=16 * 1024 * 1024),
        name=name,
    )(*scalars, *[pltpu.with_memory_space_constraint(x, pltpu.VMEM) for x in ins])


def masked(probe, rank):
    slots = lax.broadcasted_iota(jnp.int32, probe.shape, 0)
    return jnp.where(slots < rank, probe, 0.0).astype(BF16)


def sketch_kernel(ranks, v_ref, u_ref, sketch_ref, send_ref, keep_ref):
    x, core = place()
    for k in range(NX):
        for other in range(2):
            tile = ((x + k) & 3) + 4 * (core ^ other)
            probe = masked(dot(v_ref[tile], sketch_ref[...], NEAR), ranks[tile])
            out = dot(probe, u_ref[tile], LEFT)
            if other:
                send_ref[k] = out.astype(BF16)
            else:
                keep_ref[k] = out


def project_kernel(ranks, u_ref, v_ref, *refs):
    bases, (send_ref, keep_ref) = refs[:NU], refs[NU:]
    x, core = place()
    for d in range(NX):
        for other in range(2):
            tile = ((x - d) & 3) + 4 * (core ^ other)
            basis = bases[NX * other + d][...]
            coeff = masked(dot(u_ref[tile], basis, NEAR), ranks[tile])
            out = dot(coeff, v_ref[tile], LEFT)
            if other:
                send_ref[-d % NX] = out.astype(BF16)
            else:
                keep_ref[-d % NX] = out


def pair_sum_kernel(keep_ref, got_ref, own_ref, a_ref, b_ref, c_ref):
    for k, ref in enumerate((own_ref, a_ref, b_ref, c_ref)):
        ref[...] = (keep_ref[k] + got_ref[k].astype(F32)).astype(ref.dtype)


def owner_parts(send, keep):
    got = perm(send, partner)
    shape = keep.shape[1:]
    own, *others = call(
        pair_sum_kernel, "pair_sum", [(shape, F32)] + [(shape, BF16)] * 3, [keep, got]
    )
    return [own] + [perm(part, along_x(k + 1)) for k, part in enumerate(others)]


def owner_sum(own_ref, *others):
    total = own_ref[...]
    for ref in others:
        total = total + ref[...].astype(F32)
    return total


def basis_kernel(own_ref, a_ref, b_ref, c_ref, basis_ref):
    summed = owner_sum(own_ref, a_ref, b_ref, c_ref)
    rk = summed.shape[0]
    gram = dot(summed, summed, NEAR, EXACT)
    rows = lax.broadcasted_iota(jnp.int32, (rk, rk), 0)
    cols = lax.broadcasted_iota(jnp.int32, (rk, rk), 1)
    row_at = lax.broadcasted_iota(jnp.int32, (rk, 1), 0)
    work = jnp.concatenate([gram, jnp.where(rows == cols, 1.0, 0.0)], axis=1)
    for k in range(0, rk, 2):
        first, second = work[k : k + 1, :], work[k + 1 : k + 2, :]
        a, b = first[:, k : k + 1], first[:, k + 1 : k + 2]
        ratio = b / a
        second = second - ratio * first
        rest = second[:, k + 1 : k + 2]
        below = row_at > k + 1
        col = jnp.where(below, work[:, k : k + 1], 0.0)
        col_next = jnp.where(below, work[:, k + 1 : k + 2], 0.0) - ratio * col
        work = work - col * (first * (1.0 / a)) - col_next * (second * (1.0 / rest))
    left, right = work[:, :rk], work[:, rk:]
    odd = (row_at & 1) == 1
    on_diag = jnp.sum(jnp.where(rows == cols, left, 0.0), axis=1, keepdims=True)
    beside = jnp.where(rows == (cols ^ 1), left, 0.0)
    off_diag = jnp.sum(beside, axis=1, keepdims=True)
    partner_diag = jnp.sum(
        jnp.where(rows == (cols ^ 1), jnp.sum(jnp.where(rows == cols, left, 0.0), axis=0, keepdims=True), 0.0),
        axis=1,
        keepdims=True,
    )
    ratio = jnp.where(odd, off_diag / partner_diag, 0.0)
    scale = lax.rsqrt(on_diag - ratio * off_diag)
    pivot = jnp.where(rows == cols, scale, 0.0) - jnp.where(rows == (cols ^ 1), ratio * scale, 0.0)
    inverse = dot(pivot, right, ((1,), (0,)), EXACT)
    basis_ref[...] = dot(inverse, summed, ((1,), (0,)), EXACT).astype(BF16)


def cross_kernel(own_ref, a_ref, b_ref, c_ref, cross_ref):
    cross_ref[...] = owner_sum(own_ref, a_ref, b_ref, c_ref).astype(BF16)


def at_owner(kernel, name, parts):
    return call(kernel, name, [(parts[0].shape, BF16)], parts)[0]


def gathered(own):
    mine = [own] + [perm(own, along_x(d)) for d in range(1, NX)]
    return mine + [perm(block, partner) for block in mine]


def split_kernel(panel_ref, send_ref, keep_ref):
    x, core = place()
    for k in range(NX):
        tile = (x + k) & 3
        send_ref[k] = panel_ref[tile + 4 * (core ^ 1)]
        keep_ref[k] = panel_ref[tile + 4 * core]


def bundle_kernel(keep_ref, got_ref, *outs):
    for k, ref in enumerate(outs):
        ref[0] = keep_ref[NX - len(outs) + k]
        ref[1] = got_ref[NX - len(outs) + k]


def bundles(keep, got, first):
    shape = ((2,) + keep.shape[1:], BF16)
    return call(bundle_kernel, "bundle", [shape] * (NX - first), [keep, got])


def whole_tile_rows(panel):
    shape = ((NX,) + panel.shape[1:], BF16)
    send, keep = call(split_kernel, "split_panel", [shape] * 2, [panel])
    got = perm(send, partner)
    out = bundles(keep, got, 1)
    return [keep, got] + [perm(block, along_x(k + 1)) for k, block in enumerate(out)]


def tile_kernel(basis_ref, cross_ref, dinv_ref, keep_ref, got_ref, a_ref, b_ref, c_ref, send_out, keep_out, updated, solved):
    x, core = place()
    lowrank = dot(basis_ref[...], cross_ref[...], LEFT)
    updated[...] = lowrank
    for d in range(NX):
        for other in range(2):
            at = pl.multiple_of((2 * ((x - d) & 3) + (core ^ other)) * BLK, BLK)
            if d:
                rows = (a_ref, b_ref, c_ref)[d - 1][other]
            else:
                rows = (keep_ref, got_ref)[other][0]
            updated[pl.ds(at, BLK)] = rows.astype(F32) - updated[pl.ds(at, BLK)]
    wrap = (HALF - 1) * BLK
    result = dot(updated[...].astype(BF16), dinv_ref[...], NEAR).astype(BF16)
    solved[wrap:] = result
    solved[:wrap] = result[-wrap:]
    for k in range(NX):
        at = pl.multiple_of(((x + k) & 3) * (2 * BLK), 2 * BLK)
        product = dot(solved[pl.ds(at + wrap, 2 * BLK)], solved[pl.ds(at, (HALF + 1) * BLK)], NEAR)
        upper = product[:BLK, : HALF * BLK].astype(BF16)
        lower = product[BLK:, BLK:].astype(BF16)
        on_lower = core == 1
        keep_out[k] = jnp.where(on_lower, lower, upper)
        send_out[k] = jnp.where(on_lower, upper, lower)


def tile_call(basis, cross, dinv, rows):
    width = dinv.shape[0]
    out = ((NX, BLK, HALF * BLK), BF16)
    return call(
        tile_kernel,
        "tile_product",
        [out, out],
        [basis, cross, dinv, *rows],
        scratch=[
            pltpu.VMEM((width, width), F32),
            pltpu.VMEM((width + (HALF - 1) * BLK, width), BF16),
        ],
    )


def rows_kernel(panel_ref, dinv_ref, *refs):
    bases, crosses = refs[:NU], refs[NU : 2 * NU]
    out_ref, updated, solved, sems = refs[2 * NU :]
    x, core = place()
    at = pl.multiple_of((2 * x + core) * BLK, BLK)
    copies = []
    for d in range(NX):
        for other in range(2):
            tile = ((x - d) & 3) + 4 * (core ^ other)
            source = NX * other + d
            lowrank = dot(bases[source][:, pl.ds(at, BLK)], crosses[source][...], LEFT)
            rows = (panel_ref[tile].astype(F32) - lowrank).astype(BF16)
            updated[other * BLK : (other + 1) * BLK] = rows
        result = dot(updated[...], dinv_ref[...], NEAR).astype(BF16)
        for other in range(2):
            tile = ((x - d) & 3) + 4 * (core ^ other)
            slot = 2 * d + other
            solved[slot] = result[other * BLK : (other + 1) * BLK]
            copy = pltpu.make_async_copy(solved.at[slot], out_ref.at[tile], sems.at[slot])
            copy.start()
            copies.append(copy)
    for copy in copies:
        copy.wait()


def rows_call(panel, dinv, bases, crosses):
    return call(
        rows_kernel,
        "panel_rows",
        [(panel.shape, BF16)],
        [panel, dinv, *bases, *crosses],
        scratch=[
            pltpu.VMEM((2 * BLK, panel.shape[2]), BF16),
            pltpu.VMEM(panel.shape, BF16),
            pltpu.SemaphoreType.DMA((NU,)),
        ],
        in_hbm=True,
    )[0]


def arrived_kernel(a_ref, b_ref, c_ref, d_ref, here_ref, onward_ref):
    core = place()[1]
    for ref, side in ((here_ref, core), (onward_ref, core ^ 1)):
        total = a_ref[side].astype(F32)
        for block in (b_ref, c_ref, d_ref):
            total = total + block[side].astype(F32)
        ref[...] = total.astype(ref.dtype)


def collect_kernel(here_ref, onward_ref, total_ref, a_ref, b_ref, c_ref):
    total = here_ref[...] + onward_ref[...].astype(F32)
    total_ref[...] = total
    for d, ref in ((1, a_ref), (2, b_ref), (3, c_ref)):
        i = HALF - 1 - d
        ref[...] = total[:, i * BLK : (i + 1) * BLK].T


def diag_kernel(diag_ref, total_ref, a_ref, b_ref, c_ref, out_ref):
    x, core = place()
    u = 2 * x + core
    for i in range(HALF):
        at = pl.ds(pl.multiple_of(((u + i + 4) & 7) * BLK, BLK), BLK)
        out_ref[:, at] = diag_ref[:, at].astype(F32) - total_ref[:, i * BLK : (i + 1) * BLK]
    for d, ref in ((1, a_ref), (2, b_ref), (3, c_ref)):
        at = pl.ds(pl.multiple_of(((u + d) & 7) * BLK, BLK), BLK)
        out_ref[:, at] = diag_ref[:, at].astype(F32) - ref[...]


def diag_call(diag, total, mirrored):
    vmem = pl.BlockSpec(memory_space=pltpu.VMEM)
    ins = [diag, total, *mirrored]
    return pl.pallas_call(
        diag_kernel,
        out_shape=jax.ShapeDtypeStruct(diag.shape, F32),
        in_specs=[vmem] * len(ins),
        out_specs=vmem,
        compiler_params=pltpu.CompilerParams(vmem_limit_bytes=16 * 1024 * 1024),
        name="diagonal",
    )(*[pltpu.with_memory_space_constraint(x, pltpu.VMEM) for x in ins])


def local(panel, diag_tiles, dinv, u_fac, v_fac, ranks, sketch):
    panel, dinv = panel[0], dinv[0]
    u, v, ranks = u_fac[0, :, 0], v_fac[0, :, 0], ranks[0, :, 0]
    small = sketch.shape[1:]
    split = [((NX,) + small, BF16), ((NX,) + small, F32)]

    send, keep = call(sketch_kernel, "sketch_product", split, [v, u, sketch[0]], [ranks])
    parts = owner_parts(send, keep)
    rows = whole_tile_rows(panel)
    basis = at_owner(basis_kernel, "orthonormal", parts)
    bases = gathered(basis)
    send, keep = call(project_kernel, "basis_product", split, [u, v, *bases], [ranks])
    cross = at_owner(cross_kernel, "cross_sum", owner_parts(send, keep))
    send, keep = tile_call(basis, cross, dinv, rows)
    out = bundles(keep, perm(send, partner), 0)
    arrived = [perm(block, to_column(k)) for k, block in enumerate(out)]
    crosses = gathered(cross)
    shape = arrived[0].shape[1:]
    here, onward = call(arrived_kernel, "arrived_sum", [(shape, F32), (shape, BF16)], arrived)
    mirror = ((BLK, BLK), F32)
    total, *mirrored = call(
        collect_kernel, "collect", [(shape, F32)] + [mirror] * 3, [here, perm(onward, four_on)]
    )
    mirrored = [perm(block, along_upd(-d - 1)) for d, block in enumerate(mirrored)]
    panel_out = rows_call(panel, dinv, bases, crosses)
    diag_out = diag_call(diag_tiles[0], total, mirrored)
    return (panel_out[None], diag_out[None])


def solution(mesh):
    in_specs = (
        P("col", None, "upd", None),
        P("col", "upd", None),
        P("col", None, None),
        P("col", None, "upd", None, None),
        P("col", None, "upd", None, None),
        P("col", None, "upd"),
        P("col", None, None),
    )
    out_specs = (P("col", None, "upd", None), P("col", "upd", None))
    return jax.shard_map(local, mesh=mesh, in_specs=in_specs, out_specs=out_specs, check_vma=False)
```

```python
import jax
import jax.numpy as jnp
from jax import lax
from jax.experimental import pallas as pl
from jax.experimental.pallas import tpu as pltpu
from jax.sharding import PartitionSpec as P


F32 = jnp.float32
BF16 = jnp.bfloat16
AXES = ("upd", "col")
NU = 8
NX = 4
NY = 4
NC = 32
HALF = 5
BLK = 128
NEAR = ((1,), (1,))
LEFT = ((0,), (0,))
EXACT = lax.Precision.HIGHEST


def dot(a, b, dims, precision=None):
    return lax.dot_general(a, b, (dims, ((), ())), precision=precision, preferred_element_type=F32)


def place():
    at = lax.axis_index("upd")
    return at >> 1, at & 1


def perm(block, route):
    pairs = []
    for u in range(NU):
        for c in range(NC):
            to = route(u, c)
            if to is not None:
                pairs.append((u * NC + c, to[0] * NC + to[1]))
    return lax.ppermute(block, AXES, pairs)


def along_x(k):
    return lambda u, c: ((u + 2 * k) % NU, c)


def along_upd(k):
    return lambda u, c: ((u + k) % NU, c)


def partner(u, c):
    return (u ^ 1, c)


def to_column(k):
    return lambda u, c: ((u + 2 * k) % NU, c // NY * NY + (c + u // 2 + 1) % NY)


def along_z(k):
    return lambda u, c: (u, (c + NY * k) % NC)


def call(kernel, outs, ins, scalars=(), scratch=(), in_hbm=False):
    vmem = pl.BlockSpec(memory_space=pltpu.VMEM)
    if in_hbm:
        shapes = [jax.ShapeDtypeStruct(*out) for out in outs]
    else:
        shapes = [pltpu.VMEM(*out) for out in outs]
    out_spec = pl.BlockSpec(memory_space=pl.ANY) if in_hbm else vmem
    return pl.pallas_call(
        kernel,
        out_shape=shapes,
        in_specs=[pl.BlockSpec(memory_space=pltpu.SMEM)] * len(scalars) + [vmem] * len(ins),
        out_specs=[out_spec] * len(outs),
        scratch_shapes=list(scratch),
        compiler_params=pltpu.CompilerParams(vmem_limit_bytes=16 * 1024 * 1024),
    )(*scalars, *[pltpu.with_memory_space_constraint(x, pltpu.VMEM) for x in ins])


def masked(probe, rank):
    slots = lax.broadcasted_iota(jnp.int32, probe.shape, 0)
    return jnp.where(slots < rank, probe, 0.0).astype(BF16)


def sketch_kernel(ranks, v_hbm, u_hbm, sketch_hbm, send_ref, keep_ref, v_ref, u_ref, sketch_ref, sems):
    x, core = place()
    order = [(k, other) for k in range(NX) for other in (1, 0)]
    tiles = [((x + k) & 3) + 4 * (core ^ other) for k, other in order]
    first = pltpu.make_async_copy(sketch_hbm, sketch_ref, sems.at[2 * NU])
    first.start()
    copies = []
    for i, tile in enumerate(tiles):
        pair = (
            pltpu.make_async_copy(v_hbm.at[tile], v_ref.at[i], sems.at[2 * i]),
            pltpu.make_async_copy(u_hbm.at[tile], u_ref.at[i], sems.at[2 * i + 1]),
        )
        for copy in pair:
            copy.start()
        copies.append(pair)
    first.wait()
    for i, (k, other) in enumerate(order):
        copies[i][0].wait()
        probe = masked(dot(v_ref[i], sketch_ref[...], NEAR), ranks[tiles[i]])
        copies[i][1].wait()
        out = dot(probe, u_ref[i], LEFT)
        if other:
            send_ref[k] = out.astype(BF16)
        else:
            keep_ref[k] = out


def sketch_call(ranks, v, u, sketch):
    vmem = pl.BlockSpec(memory_space=pltpu.VMEM)
    hbm = pl.BlockSpec(memory_space=pltpu.HBM)
    out = (NX,) + sketch.shape
    return pl.pallas_call(
        sketch_kernel,
        out_shape=[pltpu.VMEM(out, BF16), pltpu.VMEM(out, F32)],
        in_specs=[pl.BlockSpec(memory_space=pltpu.SMEM)] + [hbm] * 3,
        out_specs=[vmem] * 2,
        scratch_shapes=[
            pltpu.VMEM(v.shape, BF16),
            pltpu.VMEM(u.shape, BF16),
            pltpu.VMEM(sketch.shape, BF16),
            pltpu.SemaphoreType.DMA((2 * NU + 1,)),
        ],
        compiler_params=pltpu.CompilerParams(vmem_limit_bytes=16 * 1024 * 1024),
        name="sketch_product",
    )(ranks, *[pltpu.with_memory_space_constraint(x, pltpu.HBM) for x in (v, u, sketch)])


def project_kernel(ranks, u_ref, v_ref, *refs):
    bases, (send_ref, keep_ref) = refs[:NU], refs[NU:]
    x, core = place()
    for d in range(NX):
        for other in range(2):
            tile = ((x - d) & 3) + 4 * (core ^ other)
            basis = bases[NX * other + d][...]
            coeff = masked(dot(u_ref[tile], basis, NEAR), ranks[tile])
            out = dot(coeff, v_ref[tile], LEFT)
            if other:
                send_ref[-d % NX] = out.astype(BF16)
            else:
                keep_ref[-d % NX] = out


def sum_product(split, ranks, u, v, sums):
    return call(project_kernel, split, [u, v, *sums], [ranks])


def pair_sum_kernel(keep_ref, got_ref, own_ref, a_ref, b_ref, c_ref):
    for k, ref in enumerate((own_ref, a_ref, b_ref, c_ref)):
        ref[...] = (keep_ref[k] + got_ref[k].astype(F32)).astype(ref.dtype)


def pair_sum(keep, got):
    shape = keep.shape[1:]
    outs = [(shape, F32)] + [(shape, BF16)] * (NX - 1)
    return call(pair_sum_kernel, outs, [keep, got])


def owner_sum(own_ref, *others):
    total = own_ref[...]
    for ref in others:
        total = total + ref[...].astype(F32)
    return total


def summed_kernel(own_ref, a_ref, b_ref, c_ref, summed_ref):
    summed_ref[...] = owner_sum(own_ref, a_ref, b_ref, c_ref).astype(BF16)


def owner_total(own, others):
    return call(summed_kernel, [(own.shape, BF16)], [own, *others])[0]


def inverse_kernel(summed_ref, inverse_ref):
    summed = summed_ref[...].astype(F32)
    rk = summed.shape[0]
    gram = dot(summed, summed, NEAR, EXACT)
    rows = lax.broadcasted_iota(jnp.int32, (rk, rk), 0)
    cols = lax.broadcasted_iota(jnp.int32, (rk, rk), 1)
    row_at = lax.broadcasted_iota(jnp.int32, (rk, 1), 0)
    work = jnp.concatenate([gram, jnp.where(rows == cols, 1.0, 0.0)], axis=1)
    for k in range(rk):
        row = work[k : k + 1, :]
        scaled = row * (1.0 / work[k : k + 1, k : k + 1])
        col = jnp.where(row_at > k, work[:, k : k + 1], 0.0)
        work = work - col * scaled
    pivots = jnp.sum(jnp.where(rows == cols, work[:, :rk], 0.0), axis=1, keepdims=True)
    half = work[:, rk:] * lax.rsqrt(pivots)
    inverse_ref[...] = dot(half, half, LEFT, EXACT)


def cross_kernel(inverse_ref, own_ref, a_ref, b_ref, c_ref, cross_ref):
    raw = owner_sum(own_ref, a_ref, b_ref, c_ref)
    cross_ref[...] = dot(inverse_ref[...], raw, ((1,), (0,)), EXACT).astype(BF16)


def gram_inverse(summed):
    rk = summed.shape[0]
    return call(inverse_kernel, [((rk, rk), F32)], [summed])[0]


def cross_total(inverse, own, others):
    return call(cross_kernel, [(own.shape, BF16)], [inverse, own, *others])[0]


def split_kernel(panel_ref, send_ref, keep_ref):
    x, core = place()
    for k in range(NX):
        tile = (x + k) & 3
        send_ref[k] = panel_ref[tile + 4 * (core ^ 1)]
        keep_ref[k] = panel_ref[tile + 4 * core]


def bundle_kernel(keep_ref, got_ref, *outs):
    for k, ref in enumerate(outs):
        ref[0] = keep_ref[NX - len(outs) + k]
        ref[1] = got_ref[NX - len(outs) + k]


def bundles(keep, got, first):
    shape = ((2,) + keep.shape[1:], BF16)
    return call(bundle_kernel, [shape] * (NX - first), [keep, got])


def split_panel(panel):
    shape = ((NX,) + panel.shape[1:], BF16)
    return call(split_kernel, [shape] * 2, [panel])


def tile_kernel(basis_ref, cross_ref, dinv_ref, keep_ref, got_ref, a_ref, b_ref, c_ref, send_out, keep_out, updated, solved):
    x, core = place()
    lowrank = dot(basis_ref[...], cross_ref[...], LEFT)
    updated[...] = lowrank
    for d in range(NX):
        for other in range(2):
            at = pl.multiple_of((2 * ((x - d) & 3) + (core ^ other)) * BLK, BLK)
            if d:
                rows = (a_ref, b_ref, c_ref)[d - 1][other]
            else:
                rows = (keep_ref, got_ref)[other][0]
            updated[pl.ds(at, BLK)] = rows.astype(F32) - updated[pl.ds(at, BLK)]
    wrap = (HALF - 1) * BLK
    result = dot(updated[...].astype(BF16), dinv_ref[...], NEAR).astype(BF16)
    solved[wrap:] = result
    solved[:wrap] = result[-wrap:]
    for k in range(NX):
        at = pl.multiple_of(((x + k) & 3) * (2 * BLK), 2 * BLK)
        product = dot(solved[pl.ds(at + wrap, 2 * BLK)], solved[pl.ds(at, (HALF + 1) * BLK)], NEAR)
        upper = product[:BLK, : HALF * BLK].astype(BF16)
        lower = product[BLK:, BLK:].astype(BF16)
        on_lower = core == 1
        keep_out[k] = jnp.where(on_lower, lower, upper)
        send_out[k] = jnp.where(on_lower, upper, lower)


def tile_call(basis, cross, dinv, rows):
    width = dinv.shape[0]
    out = ((NX, BLK, HALF * BLK), BF16)
    return call(
        tile_kernel,
        [out, out],
        [basis, cross, dinv, *rows],
        scratch=[
            pltpu.VMEM((width, width), F32),
            pltpu.VMEM((width + (HALF - 1) * BLK, width), BF16),
        ],
    )


def rows_kernel(panel_ref, dinv_ref, *refs):
    bases, crosses = refs[:NU], refs[NU : 2 * NU]
    out_ref, updated, solved, sems = refs[2 * NU :]
    x, core = place()
    at = pl.multiple_of((2 * x + core) * BLK, BLK)
    copies = []
    for d in range(NX):
        for other in range(2):
            tile = ((x - d) & 3) + 4 * (core ^ other)
            source = NX * other + d
            lowrank = dot(bases[source][:, pl.ds(at, BLK)], crosses[source][...], LEFT)
            rows = (panel_ref[tile].astype(F32) - lowrank).astype(BF16)
            updated[other * BLK : (other + 1) * BLK] = rows
        result = dot(updated[...], dinv_ref[...], NEAR).astype(BF16)
        for other in range(2):
            tile = ((x - d) & 3) + 4 * (core ^ other)
            slot = 2 * d + other
            solved[slot] = result[other * BLK : (other + 1) * BLK]
            copy = pltpu.make_async_copy(solved.at[slot], out_ref.at[tile], sems.at[slot])
            copy.start()
            copies.append(copy)
    for copy in copies:
        copy.wait()


def rows_call(panel, dinv, bases, crosses):
    return call(
        rows_kernel,
        [(panel.shape, BF16)],
        [panel, dinv, *bases, *crosses],
        scratch=[
            pltpu.VMEM((2 * BLK, panel.shape[2]), BF16),
            pltpu.VMEM(panel.shape, BF16),
            pltpu.SemaphoreType.DMA((NU,)),
        ],
        in_hbm=True,
    )[0]


def arrived_kernel(a_ref, b_ref, c_ref, d_ref, here_ref, one_ref, two_ref):
    x, core = place()
    y = lax.axis_index("col") & 3
    here = one = two = None
    for k, ref in enumerate((a_ref, b_ref, c_ref, d_ref)):
        stays = y > ((x - k) & 3)
        near, far = ref[core].astype(F32), ref[core ^ 1].astype(F32)
        parts = (jnp.where(stays, near, 0.0), jnp.where(stays, far, near), jnp.where(stays, 0.0, far))
        here, one, two = parts if k == 0 else (here + parts[0], one + parts[1], two + parts[2])
    here_ref[...] = here
    one_ref[...] = one.astype(BF16)
    two_ref[...] = two.astype(BF16)


def arrived_sum(arrived):
    shape = arrived[0].shape[1:]
    outs = [(shape, F32), (shape, BF16), (shape, BF16)]
    return call(arrived_kernel, outs, arrived)


def collect_kernel(here_ref, one_ref, two_ref, total_ref, a_ref, b_ref, c_ref):
    z = lax.axis_index("col") >> 2
    total = here_ref[...] + jnp.where(z >= 1, one_ref[...].astype(F32), 0.0)
    total = total + jnp.where(z >= 2, two_ref[...].astype(F32), 0.0)
    total_ref[...] = total
    for d, ref in ((1, a_ref), (2, b_ref), (3, c_ref)):
        i = HALF - 1 - d
        ref[...] = total[:, i * BLK : (i + 1) * BLK].T


def collect(here, onward):
    outs = [(here.shape, F32)] + [((BLK, BLK), F32)] * (HALF - 2)
    return call(collect_kernel, outs, [here, *onward])


def diag_kernel(diag_ref, total_ref, a_ref, b_ref, c_ref, out_ref):
    x, core = place()
    u = 2 * x + core
    for i in range(HALF):
        at = pl.ds(pl.multiple_of(((u + i + 4) & 7) * BLK, BLK), BLK)
        out_ref[:, at] = diag_ref[:, at].astype(F32) - total_ref[:, i * BLK : (i + 1) * BLK]
    for d, ref in ((1, a_ref), (2, b_ref), (3, c_ref)):
        at = pl.ds(pl.multiple_of(((u + d) & 7) * BLK, BLK), BLK)
        out_ref[:, at] = diag_ref[:, at].astype(F32) - ref[...]


def diag_call(diag, total, mirrored):
    vmem = pl.BlockSpec(memory_space=pltpu.VMEM)
    ins = [diag, total, *mirrored]
    return pl.pallas_call(
        diag_kernel,
        out_shape=jax.ShapeDtypeStruct(diag.shape, F32),
        in_specs=[vmem] * len(ins),
        out_specs=vmem,
        compiler_params=pltpu.CompilerParams(vmem_limit_bytes=16 * 1024 * 1024),
        name="diagonal",
    )(*[pltpu.with_memory_space_constraint(x, pltpu.VMEM) for x in ins])


def shifted(blocks, route, first=1):
    return [perm(block, route(i)) for i, block in enumerate(blocks, start=first)]


def gathered(own):
    mine = [own] + shifted([own] * (NX - 1), along_x)
    return mine + shifted(mine, lambda i: partner, 0)


def local(panel, diag_tiles, dinv, u_fac, v_fac, ranks, sketch):
    panel, dinv = panel[0], dinv[0]
    u, v, ranks = u_fac[0, :, 0], v_fac[0, :, 0], ranks[0, :, 0]
    small = sketch.shape[1:]
    split = [((NX,) + small, BF16), ((NX,) + small, F32)]

    send, keep = sketch_call(ranks, v, u, sketch[0])
    got = perm(send, partner)
    panel_send, panel_keep = split_panel(panel)
    panel_got = perm(panel_send, partner)
    own, *others = pair_sum(keep, got)
    others = shifted(others, along_x)
    panel_bundles = bundles(panel_keep, panel_got, 1)
    rows = [panel_keep, panel_got] + shifted(panel_bundles, along_x)
    own_sum = owner_total(own, others)
    sums = gathered(own_sum)
    inverse = gram_inverse(own_sum)
    send, keep = sum_product(split, ranks, u, v, sums)
    got = perm(send, partner)
    own, *others = pair_sum(keep, got)
    others = shifted(others, along_x)
    cross = cross_total(inverse, own, others)
    send, keep = tile_call(own_sum, cross, dinv, rows)
    got = perm(send, partner)
    blocks = bundles(keep, got, 0)
    arrived = shifted(blocks, to_column, 0)
    crosses = gathered(cross)
    here, *onward = arrived_sum(arrived)
    onward = shifted(onward, along_z)
    total, *mirrored = collect(here, onward)
    mirrored = shifted(mirrored, lambda d: along_upd(-d))
    panel_out = rows_call(panel, dinv, sums, crosses)
    diag_out = diag_call(diag_tiles[0], total, mirrored)
    return (panel_out[None], diag_out[None])


def solution(mesh):
    in_specs = (
        P("col", None, "upd", None),
        P("col", "upd", None),
        P("col", None, None),
        P("col", None, "upd", None, None),
        P("col", None, "upd", None, None),
        P("col", None, "upd"),
        P("col", None, None),
    )
    out_specs = (P("col", None, "upd", None), P("col", "upd", None))
    return jax.shard_map(local, mesh=mesh, in_specs=in_specs, out_specs=out_specs, check_vma=False)
```

```python
import jax
import jax.numpy as jnp
from jax import lax
from jax.experimental import pallas as pl
from jax.experimental.pallas import tpu as pltpu
from jax.sharding import PartitionSpec as P


F32 = jnp.float32
BF16 = jnp.bfloat16
AXES = ("upd", "col")
NU = 8
NX = 4
NY = 4
NZ = 8
NC = 32
HALF = 5
BLK = 128
NEAR = ((1,), (1,))
LEFT = ((0,), (0,))
EXACT = lax.Precision.HIGHEST


def dot(a, b, dims, precision=None):
    return lax.dot_general(a, b, (dims, ((), ())), precision=precision, preferred_element_type=F32)


def place():
    at = lax.axis_index("upd")
    return at >> 1, at & 1


def perm(block, route):
    pairs = []
    for u in range(NU):
        for c in range(NC):
            to = route(u, c)
            if to is not None:
                pairs.append((u * NC + c, to[0] * NC + to[1]))
    return lax.ppermute(block, AXES, pairs)


def along_x(k):
    return lambda u, c: ((u + 2 * k) % NU, c)


def along_upd(k):
    return lambda u, c: ((u + k) % NU, c)


def partner(u, c):
    return (u ^ 1, c)


def to_column(k, other):
    def route(u, c):
        x, core = u // 2, u % 2
        plane, y = c // NY, c % NY
        return (2 * ((x + k) % NX) + (core ^ other), (plane + core) % NZ * NY + (y + x + 1) % NY)

    return route


def along_z(k):
    return lambda u, c: (u, (c + NY * k) % NC)


def call(kernel, outs, ins, scalars=(), scratch=(), in_hbm=False):
    vmem = pl.BlockSpec(memory_space=pltpu.VMEM)
    if in_hbm:
        shapes = [jax.ShapeDtypeStruct(*out) for out in outs]
    else:
        shapes = [pltpu.VMEM(*out) for out in outs]
    out_spec = pl.BlockSpec(memory_space=pl.ANY) if in_hbm else vmem
    return pl.pallas_call(
        kernel,
        out_shape=shapes,
        in_specs=[pl.BlockSpec(memory_space=pltpu.SMEM)] * len(scalars) + [vmem] * len(ins),
        out_specs=[out_spec] * len(outs),
        scratch_shapes=list(scratch),
        compiler_params=pltpu.CompilerParams(vmem_limit_bytes=16 * 1024 * 1024),
    )(*scalars, *[pltpu.with_memory_space_constraint(x, pltpu.VMEM) for x in ins])


def masked(probe, rank):
    slots = lax.broadcasted_iota(jnp.int32, probe.shape, 0)
    return jnp.where(slots < rank, probe, 0.0).astype(BF16)


def sketch_kernel(ranks, v_hbm, u_hbm, sketch_hbm, send_ref, keep_ref, v_ref, u_ref, sketch_ref, sems):
    x, core = place()
    order = [(k, other) for k in range(NX) for other in (1, 0)]
    tiles = [((x + k) & 3) + 4 * (core ^ other) for k, other in order]
    first = pltpu.make_async_copy(sketch_hbm, sketch_ref, sems.at[2 * NU])
    first.start()
    copies = []
    for i, tile in enumerate(tiles):
        pair = (
            pltpu.make_async_copy(v_hbm.at[tile], v_ref.at[i], sems.at[2 * i]),
            pltpu.make_async_copy(u_hbm.at[tile], u_ref.at[i], sems.at[2 * i + 1]),
        )
        for copy in pair:
            copy.start()
        copies.append(pair)
    first.wait()
    for i, (k, other) in enumerate(order):
        copies[i][0].wait()
        probe = masked(dot(v_ref[i], sketch_ref[...], NEAR), ranks[tiles[i]])
        copies[i][1].wait()
        out = dot(probe, u_ref[i], LEFT)
        if other:
            send_ref[k] = out.astype(BF16)
        else:
            keep_ref[k] = out


def sketch_call(ranks, v, u, sketch):
    vmem = pl.BlockSpec(memory_space=pltpu.VMEM)
    hbm = pl.BlockSpec(memory_space=pltpu.HBM)
    out = (NX,) + sketch.shape
    return pl.pallas_call(
        sketch_kernel,
        out_shape=[pltpu.VMEM(out, BF16), pltpu.VMEM(out, F32)],
        in_specs=[pl.BlockSpec(memory_space=pltpu.SMEM)] + [hbm] * 3,
        out_specs=[vmem] * 2,
        scratch_shapes=[
            pltpu.VMEM(v.shape, BF16),
            pltpu.VMEM(u.shape, BF16),
            pltpu.VMEM(sketch.shape, BF16),
            pltpu.SemaphoreType.DMA((2 * NU + 1,)),
        ],
        compiler_params=pltpu.CompilerParams(vmem_limit_bytes=16 * 1024 * 1024),
        name="sketch_product",
    )(ranks, *[pltpu.with_memory_space_constraint(x, pltpu.HBM) for x in (v, u, sketch)])


def project_kernel(ranks, u_ref, v_ref, *refs):
    bases, (send_ref, keep_ref) = refs[:NU], refs[NU:]
    x, core = place()
    for d in range(NX):
        for other in range(2):
            tile = ((x - d) & 3) + 4 * (core ^ other)
            basis = bases[NX * other + d][...]
            coeff = masked(dot(u_ref[tile], basis, NEAR), ranks[tile])
            out = dot(coeff, v_ref[tile], LEFT)
            if other:
                send_ref[-d % NX] = out.astype(BF16)
            else:
                keep_ref[-d % NX] = out


def sum_product(split, ranks, u, v, sums):
    return call(project_kernel, split, [u, v, *sums], [ranks])


def pair_sum_kernel(keep_ref, got_ref, own_ref, a_ref, b_ref, c_ref):
    for k, ref in enumerate((own_ref, a_ref, b_ref, c_ref)):
        ref[...] = (keep_ref[k] + got_ref[k].astype(F32)).astype(ref.dtype)


def pair_sum(keep, got):
    shape = keep.shape[1:]
    outs = [(shape, F32)] + [(shape, BF16)] * (NX - 1)
    return call(pair_sum_kernel, outs, [keep, got])


def owner_sum(own_ref, *others):
    total = own_ref[...]
    for ref in others:
        total = total + ref[...].astype(F32)
    return total


def summed_kernel(own_ref, a_ref, b_ref, c_ref, summed_ref):
    summed_ref[...] = owner_sum(own_ref, a_ref, b_ref, c_ref).astype(BF16)


def owner_total(own, others):
    return call(summed_kernel, [(own.shape, BF16)], [own, *others])[0]


def inverse_kernel(summed_ref, inverse_ref):
    summed = summed_ref[...].astype(F32)
    rk = summed.shape[0]
    gram = dot(summed, summed, NEAR, EXACT)
    rows = lax.broadcasted_iota(jnp.int32, (rk, rk), 0)
    cols = lax.broadcasted_iota(jnp.int32, (rk, rk), 1)
    row_at = lax.broadcasted_iota(jnp.int32, (rk, 1), 0)
    work = jnp.concatenate([gram, jnp.where(rows == cols, 1.0, 0.0)], axis=1)
    for k in range(rk):
        row = work[k : k + 1, :]
        scaled = row * (1.0 / work[k : k + 1, k : k + 1])
        col = jnp.where(row_at > k, work[:, k : k + 1], 0.0)
        work = work - col * scaled
    pivots = jnp.sum(jnp.where(rows == cols, work[:, :rk], 0.0), axis=1, keepdims=True)
    half = work[:, rk:] * lax.rsqrt(pivots)
    inverse_ref[...] = dot(half, half, LEFT, EXACT)


def cross_kernel(inverse_ref, own_ref, a_ref, b_ref, c_ref, cross_ref):
    raw = owner_sum(own_ref, a_ref, b_ref, c_ref)
    cross_ref[...] = dot(inverse_ref[...], raw, ((1,), (0,)), EXACT).astype(BF16)


def gram_inverse(summed):
    rk = summed.shape[0]
    return call(inverse_kernel, [((rk, rk), F32)], [summed])[0]


def cross_total(inverse, own, others):
    return call(cross_kernel, [(own.shape, BF16)], [inverse, own, *others])[0]


def split_kernel(panel_ref, send_ref, keep_ref):
    x, core = place()
    for k in range(NX):
        tile = (x + k) & 3
        send_ref[k] = panel_ref[tile + 4 * (core ^ 1)]
        keep_ref[k] = panel_ref[tile + 4 * core]


def bundle_kernel(keep_ref, got_ref, *outs):
    for k, ref in enumerate(outs):
        ref[0] = keep_ref[NX - len(outs) + k]
        ref[1] = got_ref[NX - len(outs) + k]


def bundles(keep, got, first):
    shape = ((2,) + keep.shape[1:], BF16)
    return call(bundle_kernel, [shape] * (NX - first), [keep, got])


def split_panel(panel):
    shape = ((NX,) + panel.shape[1:], BF16)
    return call(split_kernel, [shape] * 2, [panel])


def tile_kernel(basis_ref, cross_ref, dinv_ref, keep_ref, got_ref, a_ref, b_ref, c_ref, *refs):
    outs, (updated, solved) = refs[:NU], refs[NU:]
    x, core = place()
    lowrank = dot(basis_ref[...], cross_ref[...], LEFT)
    updated[...] = lowrank
    for d in range(NX):
        for other in range(2):
            at = pl.multiple_of((2 * ((x - d) & 3) + (core ^ other)) * BLK, BLK)
            if d:
                rows = (a_ref, b_ref, c_ref)[d - 1][other]
            else:
                rows = (keep_ref, got_ref)[other][0]
            updated[pl.ds(at, BLK)] = rows.astype(F32) - updated[pl.ds(at, BLK)]
    wrap = (HALF - 1) * BLK
    result = dot(updated[...].astype(BF16), dinv_ref[...], NEAR).astype(BF16)
    solved[wrap:] = result
    solved[:wrap] = result[-wrap:]
    for k in range(NX):
        at = pl.multiple_of(((x + k) & 3) * (2 * BLK), 2 * BLK)
        product = dot(solved[pl.ds(at + wrap, 2 * BLK)], solved[pl.ds(at, (HALF + 1) * BLK)], NEAR)
        upper = product[:BLK, : HALF * BLK].astype(BF16)
        lower = product[BLK:, BLK:].astype(BF16)
        on_lower = core == 1
        outs[2 * k][...] = jnp.where(on_lower, lower, upper)
        outs[2 * k + 1][...] = jnp.where(on_lower, upper, lower)


def tile_call(basis, cross, dinv, rows):
    width = dinv.shape[0]
    out = ((BLK, HALF * BLK), BF16)
    return call(
        tile_kernel,
        [out] * NU,
        [basis, cross, dinv, *rows],
        scratch=[
            pltpu.VMEM((width, width), F32),
            pltpu.VMEM((width + (HALF - 1) * BLK, width), BF16),
        ],
    )


def rows_kernel(panel_ref, dinv_ref, *refs):
    bases, crosses = refs[:NU], refs[NU : 2 * NU]
    out_ref, updated, solved, sems = refs[2 * NU :]
    x, core = place()
    at = pl.multiple_of((2 * x + core) * BLK, BLK)
    copies = []
    for d in range(NX):
        for other in range(2):
            tile = ((x - d) & 3) + 4 * (core ^ other)
            source = NX * other + d
            lowrank = dot(bases[source][:, pl.ds(at, BLK)], crosses[source][...], LEFT)
            rows = (panel_ref[tile].astype(F32) - lowrank).astype(BF16)
            updated[other * BLK : (other + 1) * BLK] = rows
        result = dot(updated[...], dinv_ref[...], NEAR).astype(BF16)
        for other in range(2):
            tile = ((x - d) & 3) + 4 * (core ^ other)
            slot = 2 * d + other
            solved[slot] = result[other * BLK : (other + 1) * BLK]
            copy = pltpu.make_async_copy(solved.at[slot], out_ref.at[tile], sems.at[slot])
            copy.start()
            copies.append(copy)
    for copy in copies:
        copy.wait()


def rows_call(panel, dinv, bases, crosses):
    return call(
        rows_kernel,
        [(panel.shape, BF16)],
        [panel, dinv, *bases, *crosses],
        scratch=[
            pltpu.VMEM((2 * BLK, panel.shape[2]), BF16),
            pltpu.VMEM(panel.shape, BF16),
            pltpu.SemaphoreType.DMA((NU,)),
        ],
        in_hbm=True,
    )[0]


def arrived_kernel(*refs):
    refs, (here_ref, onward_ref) = refs[:NU], refs[NU:]
    x, core = place()
    col = lax.axis_index("col")
    y, z = col & 3, col >> 2
    here, onward = 0.0, 0.0
    for k in range(NX):
        first, second = refs[2 * k][...].astype(F32), refs[2 * k + 1][...].astype(F32)
        near = jnp.where(core == 0, first, second)
        far = jnp.where(core == 0, second, first)
        both = near + jnp.where(z > 0, far, 0.0)
        stays = y > ((x - k) & 3)
        here = here + jnp.where(stays, both, 0.0)
        onward = onward + jnp.where(stays, 0.0, both)
    here_ref[...] = here
    onward_ref[...] = onward.astype(BF16)


def arrived_sum(arrived):
    shape = arrived[0].shape
    return call(arrived_kernel, [(shape, F32), (shape, BF16)], arrived)


def collect_kernel(here_ref, onward_ref, total_ref, a_ref, b_ref, c_ref):
    z = lax.axis_index("col") >> 2
    total = here_ref[...] + jnp.where(z > 0, onward_ref[...].astype(F32), 0.0)
    total_ref[...] = total
    for d, ref in ((1, a_ref), (2, b_ref), (3, c_ref)):
        i = HALF - 1 - d
        ref[...] = total[:, i * BLK : (i + 1) * BLK].T


def collect(here, onward):
    outs = [(here.shape, F32)] + [((BLK, BLK), F32)] * (HALF - 2)
    return call(collect_kernel, outs, [here, *onward])


def diag_kernel(diag_ref, total_ref, a_ref, b_ref, c_ref, out_ref):
    x, core = place()
    u = 2 * x + core
    for i in range(HALF):
        at = pl.ds(pl.multiple_of(((u + i + 4) & 7) * BLK, BLK), BLK)
        out_ref[:, at] = diag_ref[:, at].astype(F32) - total_ref[:, i * BLK : (i + 1) * BLK]
    for d, ref in ((1, a_ref), (2, b_ref), (3, c_ref)):
        at = pl.ds(pl.multiple_of(((u + d) & 7) * BLK, BLK), BLK)
        out_ref[:, at] = diag_ref[:, at].astype(F32) - ref[...]


def diag_call(diag, total, mirrored):
    vmem = pl.BlockSpec(memory_space=pltpu.VMEM)
    ins = [diag, total, *mirrored]
    return pl.pallas_call(
        diag_kernel,
        out_shape=jax.ShapeDtypeStruct(diag.shape, F32),
        in_specs=[vmem] * len(ins),
        out_specs=vmem,
        compiler_params=pltpu.CompilerParams(vmem_limit_bytes=16 * 1024 * 1024),
        name="diagonal",
    )(*[pltpu.with_memory_space_constraint(x, pltpu.VMEM) for x in ins])


def shifted(blocks, route, first=1):
    return [perm(block, route(i)) for i, block in enumerate(blocks, start=first)]


def gathered(own):
    mine = [own] + shifted([own] * (NX - 1), along_x)
    return mine + shifted(mine, lambda i: partner, 0)


def local(panel, diag_tiles, dinv, u_fac, v_fac, ranks, sketch):
    panel, dinv = panel[0], dinv[0]
    u, v, ranks = u_fac[0, :, 0], v_fac[0, :, 0], ranks[0, :, 0]
    small = sketch.shape[1:]
    split = [((NX,) + small, BF16), ((NX,) + small, F32)]

    send, keep = sketch_call(ranks, v, u, sketch[0])
    got = perm(send, partner)
    panel_send, panel_keep = split_panel(panel)
    panel_got = perm(panel_send, partner)
    own, *others = pair_sum(keep, got)
    others = shifted(others, along_x)
    panel_bundles = bundles(panel_keep, panel_got, 1)
    rows = [panel_keep, panel_got] + shifted(panel_bundles, along_x)
    own_sum = owner_total(own, others)
    sums = gathered(own_sum)
    inverse = gram_inverse(own_sum)
    send, keep = sum_product(split, ranks, u, v, sums)
    got = perm(send, partner)
    own, *others = pair_sum(keep, got)
    others = shifted(others, along_x)
    cross = cross_total(inverse, own, others)
    blocks = tile_call(own_sum, cross, dinv, rows)
    arrived = shifted(blocks, lambda i: to_column(i // 2, i % 2), 0)
    crosses = gathered(cross)
    here, onward = arrived_sum(arrived)
    onward = [perm(onward, along_z(1))]
    total, *mirrored = collect(here, onward)
    mirrored = shifted(mirrored, lambda d: along_upd(-d))
    panel_out = rows_call(panel, dinv, sums, crosses)
    diag_out = diag_call(diag_tiles[0], total, mirrored)
    return (panel_out[None], diag_out[None])


def solution(mesh):
    in_specs = (
        P("col", None, "upd", None),
        P("col", "upd", None),
        P("col", None, None),
        P("col", None, "upd", None, None),
        P("col", None, "upd", None, None),
        P("col", None, "upd"),
        P("col", None, None),
    )
    out_specs = (P("col", None, "upd", None), P("col", "upd", None))
    return jax.shard_map(local, mesh=mesh, in_specs=in_specs, out_specs=out_specs, check_vma=False)
```

```python
import jax
import jax.numpy as jnp
from jax import lax
from jax.experimental import pallas as pl
from jax.experimental.pallas import tpu as pltpu
from jax.sharding import PartitionSpec as P


F32 = jnp.float32
BF16 = jnp.bfloat16
AXES = ("upd", "col")
NU = 8
NX = 4
NY = 4
NZ = 8
NC = 32
HALF = 5
BLK = 128
NEAR = ((1,), (1,))
LEFT = ((0,), (0,))
EXACT = lax.Precision.HIGHEST


def dot(a, b, dims, precision=None):
    return lax.dot_general(a, b, (dims, ((), ())), precision=precision, preferred_element_type=F32)


def place():
    at = lax.axis_index("upd")
    return at >> 1, at & 1


def perm(block, route):
    pairs = []
    for u in range(NU):
        for c in range(NC):
            to = route(u, c)
            if to is not None:
                pairs.append((u * NC + c, to[0] * NC + to[1]))
    return lax.ppermute(block, AXES, pairs)


def along_x(k):
    return lambda u, c: ((u + 2 * k) % NU, c)


def along_upd(k):
    return lambda u, c: ((u + k) % NU, c)


def partner(u, c):
    return (u ^ 1, c)


def to_column(k, other):
    def route(u, c):
        x, core = u // 2, u % 2
        plane, y = c // NY, c % NY
        return (2 * ((x + k) % NX) + (core ^ other), (plane + core) % NZ * NY + (y + x + 1) % NY)

    return route


def along_z(k):
    return lambda u, c: (u, (c + NY * k) % NC)


def call(kernel, outs, ins, scalars=(), scratch=(), in_hbm=False):
    vmem = pl.BlockSpec(memory_space=pltpu.VMEM)
    if in_hbm:
        shapes = [jax.ShapeDtypeStruct(*out) for out in outs]
    else:
        shapes = [pltpu.VMEM(*out) for out in outs]
    out_spec = pl.BlockSpec(memory_space=pl.ANY) if in_hbm else vmem
    return pl.pallas_call(
        kernel,
        out_shape=shapes,
        in_specs=[pl.BlockSpec(memory_space=pltpu.SMEM)] * len(scalars) + [vmem] * len(ins),
        out_specs=[out_spec] * len(outs),
        scratch_shapes=list(scratch),
        compiler_params=pltpu.CompilerParams(vmem_limit_bytes=16 * 1024 * 1024),
    )(*scalars, *[pltpu.with_memory_space_constraint(x, pltpu.VMEM) for x in ins])


def masked(probe, rank):
    slots = lax.broadcasted_iota(jnp.int32, probe.shape, 0)
    return jnp.where(slots < rank, probe, 0.0).astype(BF16)


def sketch_kernel(ranks, v_hbm, u_hbm, sketch_hbm, send_ref, keep_ref, v_ref, u_ref, sketch_ref, sems):
    x, core = place()
    order = [(k, other) for k in range(NX) for other in (1, 0)]
    tiles = [((x + k) & 3) + 4 * (core ^ other) for k, other in order]
    first = pltpu.make_async_copy(sketch_hbm, sketch_ref, sems.at[2 * NU])
    first.start()
    copies = []
    for i, tile in enumerate(tiles):
        pair = (
            pltpu.make_async_copy(v_hbm.at[tile], v_ref.at[i], sems.at[2 * i]),
            pltpu.make_async_copy(u_hbm.at[tile], u_ref.at[i], sems.at[2 * i + 1]),
        )
        for copy in pair:
            copy.start()
        copies.append(pair)
    first.wait()
    for i, (k, other) in enumerate(order):
        copies[i][0].wait()
        probe = masked(dot(v_ref[i], sketch_ref[...], NEAR), ranks[tiles[i]])
        copies[i][1].wait()
        out = dot(probe, u_ref[i], LEFT)
        if other:
            send_ref[k] = out.astype(BF16)
        else:
            keep_ref[k] = out


def sketch_call(ranks, v, u, sketch):
    vmem = pl.BlockSpec(memory_space=pltpu.VMEM)
    hbm = pl.BlockSpec(memory_space=pltpu.HBM)
    out = (NX,) + sketch.shape
    return pl.pallas_call(
        sketch_kernel,
        out_shape=[pltpu.VMEM(out, BF16), pltpu.VMEM(out, F32)],
        in_specs=[pl.BlockSpec(memory_space=pltpu.SMEM)] + [hbm] * 3,
        out_specs=[vmem] * 2,
        scratch_shapes=[
            pltpu.VMEM(v.shape, BF16),
            pltpu.VMEM(u.shape, BF16),
            pltpu.VMEM(sketch.shape, BF16),
            pltpu.SemaphoreType.DMA((2 * NU + 1,)),
        ],
        compiler_params=pltpu.CompilerParams(vmem_limit_bytes=16 * 1024 * 1024),
        name="sketch_product",
    )(ranks, *[pltpu.with_memory_space_constraint(x, pltpu.HBM) for x in (v, u, sketch)])


def project_kernel(ranks, u_ref, v_ref, *refs):
    bases, (send_ref, keep_ref) = refs[:NU], refs[NU:]
    x, core = place()
    for d in range(NX):
        for other in range(2):
            tile = ((x - d) & 3) + 4 * (core ^ other)
            basis = bases[NX * other + d][...]
            coeff = masked(dot(u_ref[tile], basis, NEAR), ranks[tile])
            out = dot(coeff, v_ref[tile], LEFT)
            if other:
                send_ref[-d % NX] = out.astype(BF16)
            else:
                keep_ref[-d % NX] = out


def sum_product(split, ranks, u, v, sums):
    return call(project_kernel, split, [u, v, *sums], [ranks])


def pair_sum_kernel(keep_ref, got_ref, own_ref, a_ref, b_ref, c_ref):
    for k, ref in enumerate((own_ref, a_ref, b_ref, c_ref)):
        ref[...] = (keep_ref[k] + got_ref[k].astype(F32)).astype(ref.dtype)


def pair_sum(keep, got):
    shape = keep.shape[1:]
    outs = [(shape, F32)] + [(shape, BF16)] * (NX - 1)
    return call(pair_sum_kernel, outs, [keep, got])


def owner_sum(own_ref, *others):
    total = own_ref[...]
    for ref in others:
        total = total + ref[...].astype(F32)
    return total


def summed_kernel(own_ref, a_ref, b_ref, c_ref, summed_ref):
    summed_ref[...] = owner_sum(own_ref, a_ref, b_ref, c_ref).astype(BF16)


def owner_total(own, others):
    return call(summed_kernel, [(own.shape, BF16)], [own, *others])[0]


def inverse_kernel(summed_ref, inverse_ref):
    summed = summed_ref[...].astype(F32)
    rk = summed.shape[0]
    gram = dot(summed, summed, NEAR, EXACT)
    rows = lax.broadcasted_iota(jnp.int32, (rk, rk), 0)
    cols = lax.broadcasted_iota(jnp.int32, (rk, rk), 1)
    row_at = lax.broadcasted_iota(jnp.int32, (rk, 1), 0)
    work = jnp.concatenate([gram, jnp.where(rows == cols, 1.0, 0.0)], axis=1)
    for k in range(rk):
        row = work[k : k + 1, :]
        scaled = row * (1.0 / work[k : k + 1, k : k + 1])
        col = jnp.where(row_at > k, work[:, k : k + 1], 0.0)
        work = work - col * scaled
    pivots = jnp.sum(jnp.where(rows == cols, work[:, :rk], 0.0), axis=1, keepdims=True)
    half = work[:, rk:] * lax.rsqrt(pivots)
    inverse_ref[...] = dot(half, half, LEFT, EXACT)


def cross_kernel(inverse_ref, own_ref, a_ref, b_ref, c_ref, cross_ref):
    raw = owner_sum(own_ref, a_ref, b_ref, c_ref)
    cross_ref[...] = dot(inverse_ref[...], raw, ((1,), (0,)), EXACT).astype(BF16)


def gram_inverse(summed):
    rk = summed.shape[0]
    return call(inverse_kernel, [((rk, rk), F32)], [summed])[0]


def cross_total(inverse, own, others):
    return call(cross_kernel, [(own.shape, BF16)], [inverse, own, *others])[0]


def split_kernel(panel_ref, send_ref, keep_ref):
    x, core = place()
    for k in range(NX):
        tile = (x + k) & 3
        send_ref[k] = panel_ref[tile + 4 * (core ^ 1)]
        keep_ref[k] = panel_ref[tile + 4 * core]


def bundle_kernel(keep_ref, got_ref, *outs):
    for k, ref in enumerate(outs):
        ref[0] = keep_ref[NX - len(outs) + k]
        ref[1] = got_ref[NX - len(outs) + k]


def bundles(keep, got, first):
    shape = ((2,) + keep.shape[1:], BF16)
    return call(bundle_kernel, [shape] * (NX - first), [keep, got])


def split_panel(panel):
    shape = ((NX,) + panel.shape[1:], BF16)
    return call(split_kernel, [shape] * 2, [panel])


def tile_kernel(basis_ref, cross_ref, dinv_ref, keep_ref, got_ref, a_ref, b_ref, c_ref, *refs):
    outs, (updated, solved) = refs[:NU], refs[NU:]
    x, core = place()
    lowrank = dot(basis_ref[...], cross_ref[...], LEFT)
    updated[...] = lowrank
    for d in range(NX):
        for other in range(2):
            at = pl.multiple_of((2 * ((x - d) & 3) + (core ^ other)) * BLK, BLK)
            if d:
                rows = (a_ref, b_ref, c_ref)[d - 1][other]
            else:
                rows = (keep_ref, got_ref)[other][0]
            updated[pl.ds(at, BLK)] = rows.astype(F32) - updated[pl.ds(at, BLK)]
    wrap = (HALF - 1) * BLK
    result = dot(updated[...].astype(BF16), dinv_ref[...], NEAR).astype(BF16)
    solved[wrap:] = result
    solved[:wrap] = result[-wrap:]
    for k in range(NX):
        at = pl.multiple_of(((x + k) & 3) * (2 * BLK), 2 * BLK)
        product = dot(solved[pl.ds(at + wrap, 2 * BLK)], solved[pl.ds(at, (HALF + 1) * BLK)], NEAR)
        upper = product[:BLK, : HALF * BLK].astype(BF16)
        lower = product[BLK:, BLK:].astype(BF16)
        on_lower = core == 1
        outs[2 * k][...] = jnp.where(on_lower, lower, upper)
        outs[2 * k + 1][...] = jnp.where(on_lower, upper, lower)


def tile_call(basis, cross, dinv, rows):
    width = dinv.shape[0]
    out = ((BLK, HALF * BLK), BF16)
    return call(
        tile_kernel,
        [out] * NU,
        [basis, cross, dinv, *rows],
        scratch=[
            pltpu.VMEM((width, width), F32),
            pltpu.VMEM((width + (HALF - 1) * BLK, width), BF16),
        ],
    )


def rows_kernel(panel_ref, dinv_ref, *refs):
    bases, crosses = refs[:NU], refs[NU : 2 * NU]
    out_ref, updated, solved, sems = refs[2 * NU :]
    x, core = place()
    at = pl.multiple_of((2 * x + core) * BLK, BLK)
    copies = []
    for d in range(NX):
        for other in range(2):
            tile = ((x - d) & 3) + 4 * (core ^ other)
            source = NX * other + d
            lowrank = dot(bases[source][:, pl.ds(at, BLK)], crosses[source][...], LEFT)
            rows = (panel_ref[tile].astype(F32) - lowrank).astype(BF16)
            updated[other * BLK : (other + 1) * BLK] = rows
        result = dot(updated[...], dinv_ref[...], NEAR).astype(BF16)
        for other in range(2):
            tile = ((x - d) & 3) + 4 * (core ^ other)
            slot = 2 * d + other
            solved[slot] = result[other * BLK : (other + 1) * BLK]
            copy = pltpu.make_async_copy(solved.at[slot], out_ref.at[tile], sems.at[slot])
            copy.start()
            copies.append(copy)
    for copy in copies:
        copy.wait()


def rows_call(panel, dinv, bases, crosses):
    return call(
        rows_kernel,
        [(panel.shape, BF16)],
        [panel, dinv, *bases, *crosses],
        scratch=[
            pltpu.VMEM((2 * BLK, panel.shape[2]), BF16),
            pltpu.VMEM(panel.shape, BF16),
            pltpu.SemaphoreType.DMA((NU,)),
        ],
        in_hbm=True,
    )[0]


def arrived_kernel(*refs):
    refs, (here_ref, onward_ref) = refs[:NU], refs[NU:]
    x, core = place()
    col = lax.axis_index("col")
    y, z = col & 3, col >> 2
    here, onward = 0.0, 0.0
    for k in range(NX):
        first, second = refs[2 * k][...].astype(F32), refs[2 * k + 1][...].astype(F32)
        near = jnp.where(core == 0, first, second)
        far = jnp.where(core == 0, second, first)
        both = near + jnp.where(z > 0, far, 0.0)
        stays = y > ((x - k) & 3)
        here = here + jnp.where(stays, both, 0.0)
        onward = onward + jnp.where(stays, 0.0, both)
    here_ref[...] = here
    onward_ref[...] = onward.astype(BF16)


def arrived_sum(arrived):
    shape = arrived[0].shape
    return call(arrived_kernel, [(shape, F32), (shape, BF16)], arrived)


def collect_kernel(here_ref, onward_ref, total_ref, a_ref, b_ref, c_ref):
    z = lax.axis_index("col") >> 2
    total = here_ref[...] + jnp.where(z > 0, onward_ref[...].astype(F32), 0.0)
    total_ref[...] = total
    for d, ref in ((1, a_ref), (2, b_ref), (3, c_ref)):
        i = HALF - 1 - d
        ref[...] = total[:, i * BLK : (i + 1) * BLK].T


def collect(here, onward):
    outs = [(here.shape, F32)] + [((BLK, BLK), F32)] * (HALF - 2)
    return call(collect_kernel, outs, [here, *onward])


def diag_kernel(diag_ref, total_ref, a_ref, b_ref, c_ref, out_ref):
    x, core = place()
    u = 2 * x + core
    for i in range(HALF):
        at = pl.ds(pl.multiple_of(((u + i + 4) & 7) * BLK, BLK), BLK)
        out_ref[:, at] = diag_ref[:, at].astype(F32) - total_ref[:, i * BLK : (i + 1) * BLK]
    for d, ref in ((1, a_ref), (2, b_ref), (3, c_ref)):
        at = pl.ds(pl.multiple_of(((u + d) & 7) * BLK, BLK), BLK)
        out_ref[:, at] = diag_ref[:, at].astype(F32) - ref[...]


def diag_call(diag, total, mirrored):
    vmem = pl.BlockSpec(memory_space=pltpu.VMEM)
    ins = [diag, total, *mirrored]
    return pl.pallas_call(
        diag_kernel,
        out_shape=jax.ShapeDtypeStruct(diag.shape, F32),
        in_specs=[vmem] * len(ins),
        out_specs=vmem,
        compiler_params=pltpu.CompilerParams(vmem_limit_bytes=16 * 1024 * 1024),
        name="diagonal",
    )(*[pltpu.with_memory_space_constraint(x, pltpu.VMEM) for x in ins])


def shifted(blocks, route, first=1):
    return [perm(block, route(i)) for i, block in enumerate(blocks, start=first)]


def gathered(own):
    mine = [own] + shifted([own] * (NX - 1), along_x)
    return mine + shifted(mine, lambda i: partner, 0)


def local(panel, diag_tiles, dinv, u_fac, v_fac, ranks, sketch):
    panel, dinv = panel[0], dinv[0]
    u, v, ranks = u_fac[0, :, 0], v_fac[0, :, 0], ranks[0, :, 0]
    small = sketch.shape[1:]
    split = [((NX,) + small, BF16), ((NX,) + small, F32)]

    send, keep = sketch_call(ranks, v, u, sketch[0])
    got = perm(send, partner)
    panel_send, panel_keep = split_panel(panel)
    panel_got = perm(panel_send, partner)
    own, *others = pair_sum(keep, got)
    others = shifted(others, along_x)
    panel_bundles = bundles(panel_keep, panel_got, 1)
    rows = [panel_keep, panel_got] + shifted(panel_bundles, along_x)
    own_sum = owner_total(own, others)
    sums = gathered(own_sum)
    inverse = gram_inverse(own_sum)
    send, keep = sum_product(split, ranks, u, v, sums)
    got = perm(send, partner)
    own, *others = pair_sum(keep, got)
    others = shifted(others, along_x)
    cross = cross_total(inverse, own, others)
    blocks = tile_call(own_sum, cross, dinv, rows)
    arrived = [None] * NU
    for i in ORDER:
        arrived[i] = perm(blocks[i], to_column(i // 2, i % 2))
    crosses = gathered(cross)
    here, onward = arrived_sum(arrived)
    onward = [perm(onward, along_z(1))]
    total, *mirrored = collect(here, onward)
    mirrored = shifted(mirrored, lambda d: along_upd(-d))
    panel_out = rows_call(panel, dinv, sums, crosses)
    diag_out = diag_call(diag_tiles[0], total, mirrored)
    return (panel_out[None], diag_out[None])


ORDER = (2, 6, 3, 7, 4, 5, 0, 1)


def solution(mesh):
    in_specs = (
        P("col", None, "upd", None),
        P("col", "upd", None),
        P("col", None, None),
        P("col", None, "upd", None, None),
        P("col", None, "upd", None, None),
        P("col", None, "upd"),
        P("col", None, None),
    )
    out_specs = (P("col", None, "upd", None), P("col", "upd", None))
    return jax.shard_map(local, mesh=mesh, in_specs=in_specs, out_specs=out_specs, check_vma=False)
```

```python
import jax
import jax.numpy as jnp
from jax import lax
from jax.experimental import pallas as pl
from jax.experimental.pallas import tpu as pltpu
from jax.sharding import PartitionSpec as P


F32 = jnp.float32
BF16 = jnp.bfloat16
AXES = ("upd", "col")
NU = 8
NX = 4
NY = 4
NZ = 8
NC = 32
HALF = 5
BLK = 128
NEAR = ((1,), (1,))
LEFT = ((0,), (0,))
EXACT = lax.Precision.HIGHEST


def dot(a, b, dims, precision=None):
    return lax.dot_general(a, b, (dims, ((), ())), precision=precision, preferred_element_type=F32)


def place():
    at = lax.axis_index("upd")
    return at >> 1, at & 1


def perm(block, route):
    pairs = []
    for u in range(NU):
        for c in range(NC):
            to = route(u, c)
            if to is not None:
                pairs.append((u * NC + c, to[0] * NC + to[1]))
    return lax.ppermute(block, AXES, pairs)


def along_x(k):
    return lambda u, c: ((u + 2 * k) % NU, c)


def along_upd(k):
    return lambda u, c: ((u + k) % NU, c)


def partner(u, c):
    return (u ^ 1, c)


def to_column(k, other):
    def route(u, c):
        x, core = u // 2, u % 2
        plane, y = c // NY, c % NY
        return (2 * ((x + k) % NX) + (core ^ other), (plane + core) % NZ * NY + (y + x + 1) % NY)

    return route


def along_z(k):
    return lambda u, c: (u, (c + NY * k) % NC)


def call(kernel, outs, ins, scalars=(), scratch=(), in_hbm=False):
    vmem = pl.BlockSpec(memory_space=pltpu.VMEM)
    if in_hbm:
        shapes = [jax.ShapeDtypeStruct(*out) for out in outs]
    else:
        shapes = [pltpu.VMEM(*out) for out in outs]
    out_spec = pl.BlockSpec(memory_space=pl.ANY) if in_hbm else vmem
    return pl.pallas_call(
        kernel,
        out_shape=shapes,
        in_specs=[pl.BlockSpec(memory_space=pltpu.SMEM)] * len(scalars) + [vmem] * len(ins),
        out_specs=[out_spec] * len(outs),
        scratch_shapes=list(scratch),
        compiler_params=pltpu.CompilerParams(vmem_limit_bytes=16 * 1024 * 1024),
    )(*scalars, *[pltpu.with_memory_space_constraint(x, pltpu.VMEM) for x in ins])


def masked(probe, rank):
    slots = lax.broadcasted_iota(jnp.int32, probe.shape, 0)
    return jnp.where(slots < rank, probe, 0.0).astype(BF16)


def sketch_kernel(ranks, v_hbm, u_hbm, sketch_hbm, send_ref, keep_ref, v_ref, u_ref, sketch_ref, sems):
    x, core = place()
    order = [(k, other) for k in range(NX) for other in (1, 0)]
    tiles = [((x + k) & 3) + 4 * (core ^ other) for k, other in order]
    first = pltpu.make_async_copy(sketch_hbm, sketch_ref, sems.at[2 * NU])
    first.start()
    copies = []
    for i, tile in enumerate(tiles):
        pair = (
            pltpu.make_async_copy(v_hbm.at[tile], v_ref.at[i], sems.at[2 * i]),
            pltpu.make_async_copy(u_hbm.at[tile], u_ref.at[i], sems.at[2 * i + 1]),
        )
        for copy in pair:
            copy.start()
        copies.append(pair)
    first.wait()
    for i, (k, other) in enumerate(order):
        copies[i][0].wait()
        probe = masked(dot(v_ref[i], sketch_ref[...], NEAR), ranks[tiles[i]])
        copies[i][1].wait()
        out = dot(probe, u_ref[i], LEFT)
        if other:
            send_ref[k] = out.astype(BF16)
        else:
            keep_ref[k] = out


def sketch_call(ranks, v, u, sketch):
    vmem = pl.BlockSpec(memory_space=pltpu.VMEM)
    hbm = pl.BlockSpec(memory_space=pltpu.HBM)
    out = (NX,) + sketch.shape
    return pl.pallas_call(
        sketch_kernel,
        out_shape=[pltpu.VMEM(out, BF16), pltpu.VMEM(out, F32)],
        in_specs=[pl.BlockSpec(memory_space=pltpu.SMEM)] + [hbm] * 3,
        out_specs=[vmem] * 2,
        scratch_shapes=[
            pltpu.VMEM(v.shape, BF16),
            pltpu.VMEM(u.shape, BF16),
            pltpu.VMEM(sketch.shape, BF16),
            pltpu.SemaphoreType.DMA((2 * NU + 1,)),
        ],
        compiler_params=pltpu.CompilerParams(vmem_limit_bytes=16 * 1024 * 1024),
        name="sketch_product",
    )(ranks, *[pltpu.with_memory_space_constraint(x, pltpu.HBM) for x in (v, u, sketch)])


def project_kernel(ranks, u_ref, v_ref, *refs):
    bases, (send_ref, keep_ref) = refs[:NU], refs[NU:]
    x, core = place()
    for d in range(NX):
        for other in range(2):
            tile = ((x - d) & 3) + 4 * (core ^ other)
            basis = bases[NX * other + d][...]
            coeff = masked(dot(u_ref[tile], basis, NEAR), ranks[tile])
            out = dot(coeff, v_ref[tile], LEFT)
            if other:
                send_ref[-d % NX] = out.astype(BF16)
            else:
                keep_ref[-d % NX] = out


def sum_product(split, ranks, u, v, sums):
    return call(project_kernel, split, [u, v, *sums], [ranks])


def pair_sum_kernel(keep_ref, got_ref, own_ref, a_ref, b_ref, c_ref):
    for k, ref in enumerate((own_ref, a_ref, b_ref, c_ref)):
        ref[...] = (keep_ref[k] + got_ref[k].astype(F32)).astype(ref.dtype)


def pair_sum(keep, got):
    shape = keep.shape[1:]
    outs = [(shape, F32)] + [(shape, BF16)] * (NX - 1)
    return call(pair_sum_kernel, outs, [keep, got])


def owner_sum(own_ref, *others):
    total = own_ref[...]
    for ref in others:
        total = total + ref[...].astype(F32)
    return total


def summed_kernel(own_ref, a_ref, b_ref, c_ref, summed_ref):
    summed_ref[...] = owner_sum(own_ref, a_ref, b_ref, c_ref).astype(BF16)


def owner_total(own, others):
    return call(summed_kernel, [(own.shape, BF16)], [own, *others])[0]


def inverse_kernel(summed_ref, inverse_ref):
    summed = summed_ref[...].astype(F32)
    rk = summed.shape[0]
    gram = dot(summed, summed, NEAR, EXACT)
    rows = lax.broadcasted_iota(jnp.int32, (rk, rk), 0)
    cols = lax.broadcasted_iota(jnp.int32, (rk, rk), 1)
    row_at = lax.broadcasted_iota(jnp.int32, (rk, 1), 0)
    work = jnp.concatenate([gram, jnp.where(rows == cols, 1.0, 0.0)], axis=1)
    for k in range(rk):
        row = work[k : k + 1, :]
        scaled = row * (1.0 / work[k : k + 1, k : k + 1])
        col = jnp.where(row_at > k, work[:, k : k + 1], 0.0)
        work = work - col * scaled
    pivots = jnp.sum(jnp.where(rows == cols, work[:, :rk], 0.0), axis=1, keepdims=True)
    half = work[:, rk:] * lax.rsqrt(pivots)
    inverse_ref[...] = dot(half, half, LEFT, EXACT)


def gram_inverse(summed):
    rk = summed.shape[0]
    return call(inverse_kernel, [((rk, rk), F32)], [summed])[0]


def split_kernel(panel_ref, send_ref, keep_ref):
    x, core = place()
    for k in range(NX):
        tile = (x + k) & 3
        send_ref[k] = panel_ref[tile + 4 * (core ^ 1)]
        keep_ref[k] = panel_ref[tile + 4 * core]


def bundle_kernel(keep_ref, got_ref, *outs):
    for k, ref in enumerate(outs):
        ref[0] = keep_ref[NX - len(outs) + k]
        ref[1] = got_ref[NX - len(outs) + k]


def bundles(keep, got, first):
    shape = ((2,) + keep.shape[1:], BF16)
    return call(bundle_kernel, [shape] * (NX - first), [keep, got])


def split_panel(panel):
    shape = ((NX,) + panel.shape[1:], BF16)
    return call(split_kernel, [shape] * 2, [panel])


def tile_kernel(sum_ref, inverse_ref, own_ref, a_ref, b_ref, c_ref, dinv_ref, *refs):
    bundles, cross_ref, outs = refs[:5], refs[5], refs[6 : 6 + NU]
    updated, solved = refs[6 + NU :]
    x, core = place()
    raw = owner_sum(own_ref, a_ref, b_ref, c_ref)
    cross_ref[...] = dot(inverse_ref[...], raw, ((1,), (0,)), EXACT).astype(BF16)
    wrap = (HALF - 1) * BLK
    for d in range(NX):
        pair = ((x - d) & 3) * (2 * BLK)
        for other in range(2):
            part = (core ^ other) * BLK
            at = pl.multiple_of(pair + part, BLK)
            rows = bundles[d + 1][other] if d else bundles[other][0]
            lowrank = dot(sum_ref[:, pl.ds(at, BLK)], cross_ref[...], LEFT)
            row_block = (rows.astype(F32) - lowrank).astype(BF16)
            updated[d, pl.ds(pl.multiple_of(part, BLK), BLK)] = row_block
        result = dot(updated[d], dinv_ref[...], NEAR).astype(BF16)
        solved[pl.ds(pl.multiple_of(pair + wrap, 2 * BLK), 2 * BLK)] = result
    solved[:wrap] = solved[-wrap:]
    for k in range(NX):
        at = pl.multiple_of(((x + k) & 3) * (2 * BLK), 2 * BLK)
        product = dot(solved[pl.ds(at + wrap, 2 * BLK)], solved[pl.ds(at, (HALF + 1) * BLK)], NEAR)
        upper = product[:BLK, : HALF * BLK].astype(BF16)
        lower = product[BLK:, BLK:].astype(BF16)
        on_lower = core == 1
        outs[2 * k][...] = jnp.where(on_lower, lower, upper)
        outs[2 * k + 1][...] = jnp.where(on_lower, upper, lower)


def tile_call(summed, inverse, parts, dinv, rows):
    width = dinv.shape[0]
    out = ((BLK, HALF * BLK), BF16)
    return call(
        tile_kernel,
        [(summed.shape, BF16)] + [out] * NU,
        [summed, inverse, *parts, dinv, *rows],
        scratch=[
            pltpu.VMEM((NX, 2 * BLK, width), BF16),
            pltpu.VMEM((width + (HALF - 1) * BLK, width), BF16),
        ],
    )


def rows_kernel(panel_ref, dinv_ref, *refs):
    bases, crosses = refs[:NU], refs[NU : 2 * NU]
    out_ref, updated, solved, sems = refs[2 * NU :]
    x, core = place()
    at = pl.multiple_of((2 * x + core) * BLK, BLK)
    copies = []
    for d in range(NX):
        for other in range(2):
            tile = ((x - d) & 3) + 4 * (core ^ other)
            source = NX * other + d
            lowrank = dot(bases[source][:, pl.ds(at, BLK)], crosses[source][...], LEFT)
            rows = (panel_ref[tile].astype(F32) - lowrank).astype(BF16)
            updated[other * BLK : (other + 1) * BLK] = rows
        result = dot(updated[...], dinv_ref[...], NEAR).astype(BF16)
        for other in range(2):
            tile = ((x - d) & 3) + 4 * (core ^ other)
            slot = 2 * d + other
            solved[slot] = result[other * BLK : (other + 1) * BLK]
            copy = pltpu.make_async_copy(solved.at[slot], out_ref.at[tile], sems.at[slot])
            copy.start()
            copies.append(copy)
    for copy in copies:
        copy.wait()


def rows_call(panel, dinv, bases, crosses):
    return call(
        rows_kernel,
        [(panel.shape, BF16)],
        [panel, dinv, *bases, *crosses],
        scratch=[
            pltpu.VMEM((2 * BLK, panel.shape[2]), BF16),
            pltpu.VMEM(panel.shape, BF16),
            pltpu.SemaphoreType.DMA((NU,)),
        ],
        in_hbm=True,
    )[0]


def arrived_kernel(*refs):
    refs, (here_ref, onward_ref) = refs[:NU], refs[NU:]
    x, core = place()
    col = lax.axis_index("col")
    y, z = col & 3, col >> 2
    here, onward = 0.0, 0.0
    for k in range(NX):
        first, second = refs[2 * k][...].astype(F32), refs[2 * k + 1][...].astype(F32)
        near = jnp.where(core == 0, first, second)
        far = jnp.where(core == 0, second, first)
        both = near + jnp.where(z > 0, far, 0.0)
        stays = y > ((x - k) & 3)
        here = here + jnp.where(stays, both, 0.0)
        onward = onward + jnp.where(stays, 0.0, both)
    here_ref[...] = here
    onward_ref[...] = onward.astype(BF16)


def arrived_sum(arrived):
    shape = arrived[0].shape
    return call(arrived_kernel, [(shape, F32), (shape, BF16)], arrived)


def collect_kernel(here_ref, onward_ref, total_ref, a_ref, b_ref, c_ref):
    z = lax.axis_index("col") >> 2
    total = here_ref[...] + jnp.where(z > 0, onward_ref[...].astype(F32), 0.0)
    total_ref[...] = total
    for d, ref in ((1, a_ref), (2, b_ref), (3, c_ref)):
        i = HALF - 1 - d
        ref[...] = total[:, i * BLK : (i + 1) * BLK].T.astype(BF16)


def collect(here, onward):
    outs = [(here.shape, F32)] + [((BLK, BLK), BF16)] * (HALF - 2)
    return call(collect_kernel, outs, [here, *onward])


def diag_kernel(diag_ref, total_ref, a_ref, b_ref, c_ref, out_ref):
    x, core = place()
    u = 2 * x + core
    for i in range(HALF):
        at = pl.ds(pl.multiple_of(((u + i + 4) & 7) * BLK, BLK), BLK)
        out_ref[:, at] = diag_ref[:, at].astype(F32) - total_ref[:, i * BLK : (i + 1) * BLK]
    for d, ref in ((1, a_ref), (2, b_ref), (3, c_ref)):
        at = pl.ds(pl.multiple_of(((u + d) & 7) * BLK, BLK), BLK)
        out_ref[:, at] = diag_ref[:, at].astype(F32) - ref[...].astype(F32)


def diag_call(diag, total, mirrored):
    vmem = pl.BlockSpec(memory_space=pltpu.VMEM)
    ins = [diag, total, *mirrored]
    return pl.pallas_call(
        diag_kernel,
        out_shape=jax.ShapeDtypeStruct(diag.shape, F32),
        in_specs=[vmem] * len(ins),
        out_specs=vmem,
        compiler_params=pltpu.CompilerParams(vmem_limit_bytes=16 * 1024 * 1024),
        name="diagonal",
    )(*[pltpu.with_memory_space_constraint(x, pltpu.VMEM) for x in ins])


def shifted(blocks, route, first=1):
    return [perm(block, route(i)) for i, block in enumerate(blocks, start=first)]


def gathered(own):
    mine = [own] + shifted([own] * (NX - 1), along_x)
    return mine + shifted(mine, lambda i: partner, 0)


def local(panel, diag_tiles, dinv, u_fac, v_fac, ranks, sketch):
    panel, dinv = panel[0], dinv[0]
    u, v, ranks = u_fac[0, :, 0], v_fac[0, :, 0], ranks[0, :, 0]
    small = sketch.shape[1:]
    split = [((NX,) + small, BF16), ((NX,) + small, F32)]

    send, keep = sketch_call(ranks, v, u, sketch[0])
    got = perm(send, partner)
    panel_send, panel_keep = split_panel(panel)
    panel_got = perm(panel_send, partner)
    own, *others = pair_sum(keep, got)
    others = shifted(others, along_x)
    panel_bundles = bundles(panel_keep, panel_got, 1)
    rows = [panel_keep, panel_got] + shifted(panel_bundles, along_x)
    own_sum = owner_total(own, others)
    sums = gathered(own_sum)
    inverse = gram_inverse(own_sum)
    send, keep = sum_product(split, ranks, u, v, sums)
    got = perm(send, partner)
    own, *others = pair_sum(keep, got)
    others = shifted(others, along_x)
    tile = tile_call(own_sum, inverse, [own, *others], dinv, rows)
    cross, *blocks = tile
    arrived = [None] * NU
    for i in ORDER:
        arrived[i] = perm(blocks[i], to_column(i // 2, i % 2))
    crosses = gathered(cross)
    here, onward = arrived_sum(arrived)
    onward = [perm(onward, along_z(1))]
    total, *mirrored = collect(here, onward)
    mirrored = shifted(mirrored, lambda d: along_upd(-d))
    panel_out = rows_call(panel, dinv, sums, crosses)
    diag_out = diag_call(diag_tiles[0], total, mirrored)
    return (panel_out[None], diag_out[None])


ORDER = (2, 6, 3, 7, 4, 5, 0, 1)


def solution(mesh):
    in_specs = (
        P("col", None, "upd", None),
        P("col", "upd", None),
        P("col", None, None),
        P("col", None, "upd", None, None),
        P("col", None, "upd", None, None),
        P("col", None, "upd"),
        P("col", None, None),
    )
    out_specs = (P("col", None, "upd", None), P("col", "upd", None))
    return jax.shard_map(local, mesh=mesh, in_specs=in_specs, out_specs=out_specs, check_vma=False)
```

```python
import jax
import jax.numpy as jnp
from jax import lax
from jax.experimental import pallas as pl
from jax.experimental.pallas import tpu as pltpu
from jax.sharding import PartitionSpec as P


F32 = jnp.float32
BF16 = jnp.bfloat16
AXES = ("upd", "col")
NU = 8
NX = 4
NY = 4
NZ = 8
NC = 32
HALF = 5
BLK = 128
NEAR = ((1,), (1,))
LEFT = ((0,), (0,))
EXACT = lax.Precision.HIGHEST


def dot(a, b, dims, precision=None):
    return lax.dot_general(a, b, (dims, ((), ())), precision=precision, preferred_element_type=F32)


def place():
    at = lax.axis_index("upd")
    return at >> 1, at & 1


def perm(block, route):
    pairs = []
    for u in range(NU):
        for c in range(NC):
            to = route(u, c)
            if to is not None:
                pairs.append((u * NC + c, to[0] * NC + to[1]))
    return lax.ppermute(block, AXES, pairs)


def along_x(k):
    return lambda u, c: ((u + 2 * k) % NU, c)


def along_upd(k):
    return lambda u, c: ((u + k) % NU, c)


def partner(u, c):
    return (u ^ 1, c)


def to_column(k, other):
    def route(u, c):
        x, core = u // 2, u % 2
        plane, y = c // NY, c % NY
        return (2 * ((x + k) % NX) + (core ^ other), (plane + core) % NZ * NY + (y + x + 1) % NY)

    return route


def along_z(k):
    return lambda u, c: (u, (c + NY * k) % NC)


def call(kernel, outs, ins, scalars=(), scratch=(), in_hbm=False):
    vmem = pl.BlockSpec(memory_space=pltpu.VMEM)
    if in_hbm:
        shapes = [jax.ShapeDtypeStruct(*out) for out in outs]
    else:
        shapes = [pltpu.VMEM(*out) for out in outs]
    out_spec = pl.BlockSpec(memory_space=pl.ANY) if in_hbm else vmem
    return pl.pallas_call(
        kernel,
        out_shape=shapes,
        in_specs=[pl.BlockSpec(memory_space=pltpu.SMEM)] * len(scalars) + [vmem] * len(ins),
        out_specs=[out_spec] * len(outs),
        scratch_shapes=list(scratch),
        compiler_params=pltpu.CompilerParams(vmem_limit_bytes=16 * 1024 * 1024),
    )(*scalars, *[pltpu.with_memory_space_constraint(x, pltpu.VMEM) for x in ins])


def masked(probe, rank):
    slots = lax.broadcasted_iota(jnp.int32, probe.shape, 0)
    return jnp.where(slots < rank, probe, 0.0).astype(BF16)


def sketch_kernel(ranks, v_hbm, u_hbm, sketch_hbm, send_ref, keep_ref, v_ref, u_ref, sketch_ref, sems):
    x, core = place()
    order = [(k, other) for k in range(NX) for other in (1, 0)]
    tiles = [((x + k) & 3) + 4 * (core ^ other) for k, other in order]
    first = pltpu.make_async_copy(sketch_hbm, sketch_ref, sems.at[2 * NU])
    first.start()
    copies = []
    for i, tile in enumerate(tiles):
        pair = (
            pltpu.make_async_copy(v_hbm.at[tile], v_ref.at[i], sems.at[2 * i]),
            pltpu.make_async_copy(u_hbm.at[tile], u_ref.at[i], sems.at[2 * i + 1]),
        )
        for copy in pair:
            copy.start()
        copies.append(pair)
    first.wait()
    for i, (k, other) in enumerate(order):
        copies[i][0].wait()
        probe = masked(dot(v_ref[i], sketch_ref[...], NEAR), ranks[tiles[i]])
        copies[i][1].wait()
        out = dot(probe, u_ref[i], LEFT)
        if other:
            send_ref[k] = out.astype(BF16)
        else:
            keep_ref[k] = out


def sketch_call(ranks, v, u, sketch):
    vmem = pl.BlockSpec(memory_space=pltpu.VMEM)
    hbm = pl.BlockSpec(memory_space=pltpu.HBM)
    out = (NX,) + sketch.shape
    return pl.pallas_call(
        sketch_kernel,
        out_shape=[pltpu.VMEM(out, BF16), pltpu.VMEM(out, F32)],
        in_specs=[pl.BlockSpec(memory_space=pltpu.SMEM)] + [hbm] * 3,
        out_specs=[vmem] * 2,
        scratch_shapes=[
            pltpu.VMEM(v.shape, BF16),
            pltpu.VMEM(u.shape, BF16),
            pltpu.VMEM(sketch.shape, BF16),
            pltpu.SemaphoreType.DMA((2 * NU + 1,)),
        ],
        compiler_params=pltpu.CompilerParams(vmem_limit_bytes=16 * 1024 * 1024),
        name="sketch_product",
    )(ranks, *[pltpu.with_memory_space_constraint(x, pltpu.HBM) for x in (v, u, sketch)])


def project_kernel(ranks, u_ref, v_ref, *refs):
    bases, (send_ref, keep_ref) = refs[: NX + 1], refs[NX + 1 :]
    x, core = place()
    for d in range(NX):
        for other in range(2):
            tile = ((x - d) & 3) + 4 * (core ^ other)
            basis = from_source(bases, d, other)[...]
            coeff = masked(dot(u_ref[tile], basis, NEAR), ranks[tile])
            out = dot(coeff, v_ref[tile], LEFT)
            if other:
                send_ref[-d % NX] = out.astype(BF16)
            else:
                keep_ref[-d % NX] = out


def stack_kernel(a_ref, b_ref, c_ref, d_ref, out_ref):
    for k, ref in enumerate((a_ref, b_ref, c_ref, d_ref)):
        out_ref[k] = ref[...]


def stacked(blocks):
    return call(stack_kernel, [((NX,) + blocks[0].shape, BF16)], blocks)[0]


def from_source(refs, d, other):
    return refs[NX].at[d] if other else refs[d]


def sum_product(split, ranks, u, v, sums):
    return call(project_kernel, split, [u, v, *sums], [ranks])


def pair_sum_kernel(keep_ref, got_ref, own_ref, a_ref, b_ref, c_ref):
    for k, ref in enumerate((own_ref, a_ref, b_ref, c_ref)):
        ref[...] = (keep_ref[k] + got_ref[k].astype(F32)).astype(ref.dtype)


def pair_sum(keep, got):
    shape = keep.shape[1:]
    outs = [(shape, F32)] + [(shape, BF16)] * (NX - 1)
    return call(pair_sum_kernel, outs, [keep, got])


def owner_sum(own_ref, *others):
    total = own_ref[...]
    for ref in others:
        total = total + ref[...].astype(F32)
    return total


def summed_kernel(own_ref, a_ref, b_ref, c_ref, summed_ref):
    summed_ref[...] = owner_sum(own_ref, a_ref, b_ref, c_ref).astype(BF16)


def owner_total(own, others):
    return call(summed_kernel, [(own.shape, BF16)], [own, *others])[0]


def inverse_kernel(summed_ref, inverse_ref):
    summed = summed_ref[...].astype(F32)
    rk = summed.shape[0]
    gram = dot(summed, summed, NEAR, EXACT)
    rows = lax.broadcasted_iota(jnp.int32, (rk, rk), 0)
    cols = lax.broadcasted_iota(jnp.int32, (rk, rk), 1)
    row_at = lax.broadcasted_iota(jnp.int32, (rk, 1), 0)
    work = jnp.concatenate([gram, jnp.where(rows == cols, 1.0, 0.0)], axis=1)
    for k in range(rk):
        row = work[k : k + 1, :]
        scaled = row * (1.0 / work[k : k + 1, k : k + 1])
        col = jnp.where(row_at > k, work[:, k : k + 1], 0.0)
        work = work - col * scaled
    pivots = jnp.sum(jnp.where(rows == cols, work[:, :rk], 0.0), axis=1, keepdims=True)
    half = work[:, rk:] * lax.rsqrt(pivots)
    inverse_ref[...] = dot(half, half, LEFT, EXACT)


def gram_inverse(summed):
    rk = summed.shape[0]
    return call(inverse_kernel, [((rk, rk), F32)], [summed])[0]


def split_kernel(panel_ref, send_ref, keep_ref):
    x, core = place()
    for k in range(NX):
        tile = (x + k) & 3
        send_ref[k] = panel_ref[tile + 4 * (core ^ 1)]
        keep_ref[k] = panel_ref[tile + 4 * core]


def bundle_kernel(keep_ref, got_ref, *outs):
    for k, ref in enumerate(outs):
        ref[0] = keep_ref[NX - len(outs) + k]
        ref[1] = got_ref[NX - len(outs) + k]


def bundles(keep, got, first):
    shape = ((2,) + keep.shape[1:], BF16)
    return call(bundle_kernel, [shape] * (NX - first), [keep, got])


def split_panel(panel):
    shape = ((NX,) + panel.shape[1:], BF16)
    return call(split_kernel, [shape] * 2, [panel])


def tile_kernel(sum_ref, inverse_ref, own_ref, a_ref, b_ref, c_ref, dinv_ref, *refs):
    bundles, cross_ref, outs = refs[:5], refs[5], refs[6 : 6 + NU]
    updated, solved = refs[6 + NU :]
    x, core = place()
    raw = owner_sum(own_ref, a_ref, b_ref, c_ref)
    cross_ref[...] = dot(inverse_ref[...], raw, ((1,), (0,)), EXACT).astype(BF16)
    wrap = (HALF - 1) * BLK
    for d in range(NX):
        pair = ((x - d) & 3) * (2 * BLK)
        for other in range(2):
            part = (core ^ other) * BLK
            at = pl.multiple_of(pair + part, BLK)
            rows = bundles[d + 1][other] if d else bundles[other][0]
            lowrank = dot(sum_ref[:, pl.ds(at, BLK)], cross_ref[...], LEFT)
            row_block = (rows.astype(F32) - lowrank).astype(BF16)
            updated[d, pl.ds(pl.multiple_of(part, BLK), BLK)] = row_block
        result = dot(updated[d], dinv_ref[...], NEAR).astype(BF16)
        solved[pl.ds(pl.multiple_of(pair + wrap, 2 * BLK), 2 * BLK)] = result
    solved[:wrap] = solved[-wrap:]
    for k in range(NX):
        at = pl.multiple_of(((x + k) & 3) * (2 * BLK), 2 * BLK)
        product = dot(solved[pl.ds(at + wrap, 2 * BLK)], solved[pl.ds(at, (HALF + 1) * BLK)], NEAR)
        upper = product[:BLK, : HALF * BLK].astype(BF16)
        lower = product[BLK:, BLK:].astype(BF16)
        on_lower = core == 1
        outs[2 * k][...] = jnp.where(on_lower, lower, upper)
        outs[2 * k + 1][...] = jnp.where(on_lower, upper, lower)


def tile_call(summed, inverse, parts, dinv, rows):
    width = dinv.shape[0]
    out = ((BLK, HALF * BLK), BF16)
    return call(
        tile_kernel,
        [(summed.shape, BF16)] + [out] * NU,
        [summed, inverse, *parts, dinv, *rows],
        scratch=[
            pltpu.VMEM((NX, 2 * BLK, width), BF16),
            pltpu.VMEM((width + (HALF - 1) * BLK, width), BF16),
        ],
    )


def rows_kernel(panel_ref, dinv_ref, *refs):
    bases, crosses = refs[: NX + 1], refs[NX + 1 : 2 * NX + 2]
    out_ref, updated, solved, sems = refs[2 * NX + 2 :]
    x, core = place()
    at = pl.multiple_of((2 * x + core) * BLK, BLK)
    copies = []
    for d in range(NX):
        for other in range(2):
            tile = ((x - d) & 3) + 4 * (core ^ other)
            part = from_source(bases, d, other)[:, pl.ds(at, BLK)]
            lowrank = dot(part, from_source(crosses, d, other)[...], LEFT)
            rows = (panel_ref[tile].astype(F32) - lowrank).astype(BF16)
            updated[other * BLK : (other + 1) * BLK] = rows
        result = dot(updated[...], dinv_ref[...], NEAR).astype(BF16)
        for other in range(2):
            tile = ((x - d) & 3) + 4 * (core ^ other)
            slot = 2 * d + other
            solved[slot] = result[other * BLK : (other + 1) * BLK]
            copy = pltpu.make_async_copy(solved.at[slot], out_ref.at[tile], sems.at[slot])
            copy.start()
            copies.append(copy)
    for copy in copies:
        copy.wait()


def rows_call(panel, dinv, bases, crosses):
    return call(
        rows_kernel,
        [(panel.shape, BF16)],
        [panel, dinv, *bases, *crosses],
        scratch=[
            pltpu.VMEM((2 * BLK, panel.shape[2]), BF16),
            pltpu.VMEM(panel.shape, BF16),
            pltpu.SemaphoreType.DMA((NU,)),
        ],
        in_hbm=True,
    )[0]


def arrived_kernel(*refs):
    refs, (here_ref, onward_ref) = refs[:NU], refs[NU:]
    x, core = place()
    col = lax.axis_index("col")
    y, z = col & 3, col >> 2
    here, onward = 0.0, 0.0
    for k in range(NX):
        first, second = refs[2 * k][...].astype(F32), refs[2 * k + 1][...].astype(F32)
        near = jnp.where(core == 0, first, second)
        far = jnp.where(core == 0, second, first)
        both = near + jnp.where(z > 0, far, 0.0)
        stays = y > ((x - k) & 3)
        here = here + jnp.where(stays, both, 0.0)
        onward = onward + jnp.where(stays, 0.0, both)
    here_ref[...] = here
    onward_ref[...] = onward.astype(BF16)


def arrived_sum(arrived):
    shape = arrived[0].shape
    return call(arrived_kernel, [(shape, F32), (shape, BF16)], arrived)


def collect_kernel(here_ref, onward_ref, total_ref, a_ref, b_ref, c_ref):
    z = lax.axis_index("col") >> 2
    total = here_ref[...] + jnp.where(z > 0, onward_ref[...].astype(F32), 0.0)
    total_ref[...] = total
    for d, ref in ((1, a_ref), (2, b_ref), (3, c_ref)):
        i = HALF - 1 - d
        ref[...] = total[:, i * BLK : (i + 1) * BLK].T.astype(BF16)


def collect(here, onward):
    outs = [(here.shape, F32)] + [((BLK, BLK), BF16)] * (HALF - 2)
    return call(collect_kernel, outs, [here, *onward])


def diag_kernel(diag_ref, total_ref, a_ref, b_ref, c_ref, out_ref):
    x, core = place()
    u = 2 * x + core
    for i in range(HALF):
        at = pl.ds(pl.multiple_of(((u + i + 4) & 7) * BLK, BLK), BLK)
        out_ref[:, at] = diag_ref[:, at].astype(F32) - total_ref[:, i * BLK : (i + 1) * BLK]
    for d, ref in ((1, a_ref), (2, b_ref), (3, c_ref)):
        at = pl.ds(pl.multiple_of(((u + d) & 7) * BLK, BLK), BLK)
        out_ref[:, at] = diag_ref[:, at].astype(F32) - ref[...].astype(F32)


def diag_call(diag, total, mirrored):
    vmem = pl.BlockSpec(memory_space=pltpu.VMEM)
    ins = [diag, total, *mirrored]
    return pl.pallas_call(
        diag_kernel,
        out_shape=jax.ShapeDtypeStruct(diag.shape, F32),
        in_specs=[vmem] * len(ins),
        out_specs=vmem,
        compiler_params=pltpu.CompilerParams(vmem_limit_bytes=16 * 1024 * 1024),
        name="diagonal",
    )(*[pltpu.with_memory_space_constraint(x, pltpu.VMEM) for x in ins])


def shifted(blocks, route, first=1):
    return [perm(block, route(i)) for i, block in enumerate(blocks, start=first)]


def gathered(own):
    mine = [own] + shifted([own] * (NX - 1), along_x)
    stack = stacked(mine)
    return mine + [perm(stack, partner)]


def local(panel, diag_tiles, dinv, u_fac, v_fac, ranks, sketch):
    panel, dinv = panel[0], dinv[0]
    u, v, ranks = u_fac[0, :, 0], v_fac[0, :, 0], ranks[0, :, 0]
    small = sketch.shape[1:]
    split = [((NX,) + small, BF16), ((NX,) + small, F32)]

    send, keep = sketch_call(ranks, v, u, sketch[0])
    got = perm(send, partner)
    panel_send, panel_keep = split_panel(panel)
    panel_got = perm(panel_send, partner)
    own, *others = pair_sum(keep, got)
    others = shifted(others, along_x)
    panel_bundles = bundles(panel_keep, panel_got, 1)
    rows = [panel_keep, panel_got] + shifted(panel_bundles, along_x)
    own_sum = owner_total(own, others)
    sums = gathered(own_sum)
    inverse = gram_inverse(own_sum)
    send, keep = sum_product(split, ranks, u, v, sums)
    got = perm(send, partner)
    own, *others = pair_sum(keep, got)
    others = shifted(others, along_x)
    tile = tile_call(own_sum, inverse, [own, *others], dinv, rows)
    cross, *blocks = tile
    arrived = [None] * NU
    for i in ORDER:
        arrived[i] = perm(blocks[i], to_column(i // 2, i % 2))
    crosses = gathered(cross)
    here, onward = arrived_sum(arrived)
    onward = [perm(onward, along_z(1))]
    total, *mirrored = collect(here, onward)
    mirrored = shifted(mirrored, lambda d: along_upd(-d))
    panel_out = rows_call(panel, dinv, sums, crosses)
    diag_out = diag_call(diag_tiles[0], total, mirrored)
    return (panel_out[None], diag_out[None])


ORDER = (2, 6, 3, 7, 4, 5, 0, 1)


def solution(mesh):
    in_specs = (
        P("col", None, "upd", None),
        P("col", "upd", None),
        P("col", None, None),
        P("col", None, "upd", None, None),
        P("col", None, "upd", None, None),
        P("col", None, "upd"),
        P("col", None, None),
    )
    out_specs = (P("col", None, "upd", None), P("col", "upd", None))
    return jax.shard_map(local, mesh=mesh, in_specs=in_specs, out_specs=out_specs, check_vma=False)
```

```python
import jax
import jax.numpy as jnp
from jax import lax
from jax.experimental import pallas as pl
from jax.experimental.pallas import tpu as pltpu
from jax.sharding import PartitionSpec as P


F32 = jnp.float32
BF16 = jnp.bfloat16
AXES = ("upd", "col")
NU = 8
NX = 4
NY = 4
NZ = 8
NC = 32
HALF = 5
BLK = 128
NEAR = ((1,), (1,))
LEFT = ((0,), (0,))
EXACT = lax.Precision.HIGHEST


def dot(a, b, dims, precision=None):
    return lax.dot_general(a, b, (dims, ((), ())), precision=precision, preferred_element_type=F32)


def place():
    at = lax.axis_index("upd")
    return at >> 1, at & 1


def perm(block, route):
    pairs = []
    for u in range(NU):
        for c in range(NC):
            to = route(u, c)
            if to is not None:
                pairs.append((u * NC + c, to[0] * NC + to[1]))
    return lax.ppermute(block, AXES, pairs)


def along_x(k):
    return lambda u, c: ((u + 2 * k) % NU, c)


def along_upd(k):
    return lambda u, c: ((u + k) % NU, c)


def partner(u, c):
    return (u ^ 1, c)


def to_column(k):
    def route(u, c):
        plane, y = c // NY, c % NY
        return ((u + 2 * k) % NU, (plane + u % 2) % NZ * NY + (y + u // 2 + 1) % NY)

    return route


def along_z(k):
    return lambda u, c: (u, (c + NY * k) % NC)


def call(kernel, outs, ins, scalars=(), scratch=(), in_hbm=False):
    vmem = pl.BlockSpec(memory_space=pltpu.VMEM)
    if in_hbm:
        shapes = [jax.ShapeDtypeStruct(*out) for out in outs]
    else:
        shapes = [pltpu.VMEM(*out) for out in outs]
    out_spec = pl.BlockSpec(memory_space=pl.ANY) if in_hbm else vmem
    return pl.pallas_call(
        kernel,
        out_shape=shapes,
        in_specs=[pl.BlockSpec(memory_space=pltpu.SMEM)] * len(scalars) + [vmem] * len(ins),
        out_specs=[out_spec] * len(outs),
        scratch_shapes=list(scratch),
        compiler_params=pltpu.CompilerParams(vmem_limit_bytes=16 * 1024 * 1024),
    )(*scalars, *[pltpu.with_memory_space_constraint(x, pltpu.VMEM) for x in ins])


def masked(probe, rank):
    slots = lax.broadcasted_iota(jnp.int32, probe.shape, 0)
    return jnp.where(slots < rank, probe, 0.0).astype(BF16)


def sketch_kernel(ranks, v_hbm, u_hbm, sketch_hbm, send_ref, keep_ref, v_ref, u_ref, sketch_ref, sems):
    x, core = place()
    order = [(k, other) for k in range(NX) for other in (1, 0)]
    tiles = [((x + k) & 3) + 4 * (core ^ other) for k, other in order]
    first = pltpu.make_async_copy(sketch_hbm, sketch_ref, sems.at[2 * NU])
    first.start()
    copies = []
    for i, tile in enumerate(tiles):
        pair = (
            pltpu.make_async_copy(v_hbm.at[tile], v_ref.at[i], sems.at[2 * i]),
            pltpu.make_async_copy(u_hbm.at[tile], u_ref.at[i], sems.at[2 * i + 1]),
        )
        for copy in pair:
            copy.start()
        copies.append(pair)
    first.wait()
    for i, (k, other) in enumerate(order):
        copies[i][0].wait()
        probe = masked(dot(v_ref[i], sketch_ref[...], NEAR), ranks[tiles[i]])
        copies[i][1].wait()
        out = dot(probe, u_ref[i], LEFT)
        if other:
            send_ref[k] = out.astype(BF16)
        else:
            keep_ref[k] = out


def sketch_call(ranks, v, u, sketch):
    vmem = pl.BlockSpec(memory_space=pltpu.VMEM)
    hbm = pl.BlockSpec(memory_space=pltpu.HBM)
    out = (NX,) + sketch.shape
    return pl.pallas_call(
        sketch_kernel,
        out_shape=[pltpu.VMEM(out, BF16), pltpu.VMEM(out, F32)],
        in_specs=[pl.BlockSpec(memory_space=pltpu.SMEM)] + [hbm] * 3,
        out_specs=[vmem] * 2,
        scratch_shapes=[
            pltpu.VMEM(v.shape, BF16),
            pltpu.VMEM(u.shape, BF16),
            pltpu.VMEM(sketch.shape, BF16),
            pltpu.SemaphoreType.DMA((2 * NU + 1,)),
        ],
        compiler_params=pltpu.CompilerParams(vmem_limit_bytes=16 * 1024 * 1024),
        name="sketch_product",
    )(ranks, *[pltpu.with_memory_space_constraint(x, pltpu.HBM) for x in (v, u, sketch)])


def project_kernel(ranks, u_ref, v_ref, *refs):
    bases, (send_ref, keep_ref) = refs[: NX + 1], refs[NX + 1 :]
    x, core = place()
    for d in range(NX):
        for other in range(2):
            tile = ((x - d) & 3) + 4 * (core ^ other)
            basis = from_source(bases, d, other)[...]
            coeff = masked(dot(u_ref[tile], basis, NEAR), ranks[tile])
            out = dot(coeff, v_ref[tile], LEFT)
            if other:
                send_ref[-d % NX] = out.astype(BF16)
            else:
                keep_ref[-d % NX] = out


def stack_kernel(a_ref, b_ref, c_ref, d_ref, out_ref):
    for k, ref in enumerate((a_ref, b_ref, c_ref, d_ref)):
        out_ref[k] = ref[...]


def stacked(blocks):
    return call(stack_kernel, [((NX,) + blocks[0].shape, BF16)], blocks)[0]


def from_source(refs, d, other):
    return refs[NX].at[d] if other else refs[d]


def sum_product(split, ranks, u, v, sums):
    return call(project_kernel, split, [u, v, *sums], [ranks])


def pair_sum_kernel(keep_ref, got_ref, own_ref, a_ref, b_ref, c_ref):
    for k, ref in enumerate((own_ref, a_ref, b_ref, c_ref)):
        ref[...] = (keep_ref[k] + got_ref[k].astype(F32)).astype(ref.dtype)


def pair_sum(keep, got):
    shape = keep.shape[1:]
    outs = [(shape, F32)] + [(shape, BF16)] * (NX - 1)
    return call(pair_sum_kernel, outs, [keep, got])


def owner_sum(own_ref, *others):
    total = own_ref[...]
    for ref in others:
        total = total + ref[...].astype(F32)
    return total


def summed_kernel(own_ref, a_ref, b_ref, c_ref, summed_ref):
    summed_ref[...] = owner_sum(own_ref, a_ref, b_ref, c_ref).astype(BF16)


def owner_total(own, others):
    return call(summed_kernel, [(own.shape, BF16)], [own, *others])[0]


def inverse_kernel(summed_ref, inverse_ref):
    summed = summed_ref[...].astype(F32)
    rk = summed.shape[0]
    gram = dot(summed, summed, NEAR, EXACT)
    rows = lax.broadcasted_iota(jnp.int32, (rk, rk), 0)
    cols = lax.broadcasted_iota(jnp.int32, (rk, rk), 1)
    row_at = lax.broadcasted_iota(jnp.int32, (rk, 1), 0)
    work = jnp.concatenate([gram, jnp.where(rows == cols, 1.0, 0.0)], axis=1)
    for k in range(rk):
        row = work[k : k + 1, :]
        scaled = row * (1.0 / work[k : k + 1, k : k + 1])
        col = jnp.where(row_at > k, work[:, k : k + 1], 0.0)
        work = work - col * scaled
    pivots = jnp.sum(jnp.where(rows == cols, work[:, :rk], 0.0), axis=1, keepdims=True)
    half = work[:, rk:] * lax.rsqrt(pivots)
    inverse_ref[...] = dot(half, half, LEFT, EXACT)


def gram_inverse(summed):
    rk = summed.shape[0]
    return call(inverse_kernel, [((rk, rk), F32)], [summed])[0]


def split_kernel(panel_ref, send_ref, keep_ref):
    x, core = place()
    for k in range(NX):
        tile = (x + k) & 3
        send_ref[k] = panel_ref[tile + 4 * (core ^ 1)]
        keep_ref[k] = panel_ref[tile + 4 * core]


def bundle_kernel(keep_ref, got_ref, *outs):
    for k, ref in enumerate(outs):
        ref[0] = keep_ref[NX - len(outs) + k]
        ref[1] = got_ref[NX - len(outs) + k]


def bundles(keep, got, first):
    shape = ((2,) + keep.shape[1:], BF16)
    return call(bundle_kernel, [shape] * (NX - first), [keep, got])


def split_panel(panel):
    shape = ((NX,) + panel.shape[1:], BF16)
    return call(split_kernel, [shape] * 2, [panel])


def tile_kernel(sum_ref, inverse_ref, own_ref, a_ref, b_ref, c_ref, dinv_ref, *refs):
    bundles, cross_ref, outs = refs[:5], refs[5], refs[6 : 6 + NX]
    updated, solved = refs[6 + NX :]
    x, core = place()
    raw = owner_sum(own_ref, a_ref, b_ref, c_ref)
    cross_ref[...] = dot(inverse_ref[...], raw, ((1,), (0,)), EXACT).astype(BF16)
    wrap = (HALF - 1) * BLK
    for d in range(NX):
        pair = ((x - d) & 3) * (2 * BLK)
        for other in range(2):
            part = (core ^ other) * BLK
            at = pl.multiple_of(pair + part, BLK)
            rows = bundles[d + 1][other] if d else bundles[other][0]
            lowrank = dot(sum_ref[:, pl.ds(at, BLK)], cross_ref[...], LEFT)
            row_block = (rows.astype(F32) - lowrank).astype(BF16)
            updated[d, pl.ds(pl.multiple_of(part, BLK), BLK)] = row_block
        result = dot(updated[d], dinv_ref[...], NEAR).astype(BF16)
        solved[pl.ds(pl.multiple_of(pair + wrap, 2 * BLK), 2 * BLK)] = result
    solved[:wrap] = solved[-wrap:]
    for k in range(NX):
        at = pl.multiple_of(((x + k) & 3) * (2 * BLK), 2 * BLK)
        product = dot(solved[pl.ds(at + wrap, 2 * BLK)], solved[pl.ds(at, (HALF + 1) * BLK)], NEAR)
        outs[k][0] = product[:BLK, : HALF * BLK].astype(BF16)
        outs[k][1] = product[BLK:, BLK:].astype(BF16)


def tile_call(summed, inverse, parts, dinv, rows):
    width = dinv.shape[0]
    out = ((2, BLK, HALF * BLK), BF16)
    return call(
        tile_kernel,
        [(summed.shape, BF16)] + [out] * NX,
        [summed, inverse, *parts, dinv, *rows],
        scratch=[
            pltpu.VMEM((NX, 2 * BLK, width), BF16),
            pltpu.VMEM((width + (HALF - 1) * BLK, width), BF16),
        ],
    )


def rows_kernel(panel_ref, dinv_ref, *refs):
    bases, crosses = refs[: NX + 1], refs[NX + 1 : 2 * NX + 2]
    out_ref, updated, solved, sems = refs[2 * NX + 2 :]
    x, core = place()
    at = pl.multiple_of((2 * x + core) * BLK, BLK)
    copies = []
    for d in range(NX):
        for other in range(2):
            tile = ((x - d) & 3) + 4 * (core ^ other)
            part = from_source(bases, d, other)[:, pl.ds(at, BLK)]
            lowrank = dot(part, from_source(crosses, d, other)[...], LEFT)
            rows = (panel_ref[tile].astype(F32) - lowrank).astype(BF16)
            updated[other * BLK : (other + 1) * BLK] = rows
        result = dot(updated[...], dinv_ref[...], NEAR).astype(BF16)
        for other in range(2):
            tile = ((x - d) & 3) + 4 * (core ^ other)
            slot = 2 * d + other
            solved[slot] = result[other * BLK : (other + 1) * BLK]
            copy = pltpu.make_async_copy(solved.at[slot], out_ref.at[tile], sems.at[slot])
            copy.start()
            copies.append(copy)
    for copy in copies:
        copy.wait()


def rows_call(panel, dinv, bases, crosses):
    return call(
        rows_kernel,
        [(panel.shape, BF16)],
        [panel, dinv, *bases, *crosses],
        scratch=[
            pltpu.VMEM((2 * BLK, panel.shape[2]), BF16),
            pltpu.VMEM(panel.shape, BF16),
            pltpu.SemaphoreType.DMA((NU,)),
        ],
        in_hbm=True,
    )[0]


def arrived_kernel(a_ref, b_ref, c_ref, d_ref, send_ref, keep_ref):
    x, core = place()
    col = lax.axis_index("col")
    y, z = col & 3, col >> 2
    valid = (core == 0) | (z > 0)
    for other in range(2):
        here, onward = 0.0, 0.0
        for k, ref in enumerate((a_ref, b_ref, c_ref, d_ref)):
            block = jnp.where(valid, ref[core ^ other].astype(F32), 0.0)
            stays = y > ((x - k) & 3)
            here = here + jnp.where(stays, block, 0.0)
            onward = onward + jnp.where(stays, 0.0, block)
        if other:
            send_ref[0] = here.astype(BF16)
            send_ref[1] = onward.astype(BF16)
        else:
            keep_ref[0] = here
            keep_ref[1] = onward


def arrived_sum(arrived):
    shape = arrived[0].shape
    return call(arrived_kernel, [(shape, BF16), (shape, F32)], arrived)


def plane_kernel(keep_ref, got_ref, here_ref, onward_ref):
    here_ref[...] = keep_ref[0] + got_ref[0].astype(F32)
    onward_ref[...] = (keep_ref[1] + got_ref[1].astype(F32)).astype(BF16)


def plane_sum(keep, got):
    shape = keep.shape[1:]
    return call(plane_kernel, [(shape, F32), (shape, BF16)], [keep, got])


def collect_kernel(here_ref, onward_ref, total_ref, a_ref, b_ref, c_ref):
    z = lax.axis_index("col") >> 2
    total = here_ref[...] + jnp.where(z > 0, onward_ref[...].astype(F32), 0.0)
    total_ref[...] = total
    for d, ref in ((1, a_ref), (2, b_ref), (3, c_ref)):
        i = HALF - 1 - d
        ref[...] = total[:, i * BLK : (i + 1) * BLK].T.astype(BF16)


def collect(here, onward):
    outs = [(here.shape, F32)] + [((BLK, BLK), BF16)] * (HALF - 2)
    return call(collect_kernel, outs, [here, *onward])


def diag_kernel(diag_ref, total_ref, a_ref, b_ref, c_ref, out_ref):
    x, core = place()
    u = 2 * x + core
    for i in range(HALF):
        at = pl.ds(pl.multiple_of(((u + i + 4) & 7) * BLK, BLK), BLK)
        out_ref[:, at] = diag_ref[:, at].astype(F32) - total_ref[:, i * BLK : (i + 1) * BLK]
    for d, ref in ((1, a_ref), (2, b_ref), (3, c_ref)):
        at = pl.ds(pl.multiple_of(((u + d) & 7) * BLK, BLK), BLK)
        out_ref[:, at] = diag_ref[:, at].astype(F32) - ref[...].astype(F32)


def diag_call(diag, total, mirrored):
    vmem = pl.BlockSpec(memory_space=pltpu.VMEM)
    ins = [diag, total, *mirrored]
    return pl.pallas_call(
        diag_kernel,
        out_shape=jax.ShapeDtypeStruct(diag.shape, F32),
        in_specs=[vmem] * len(ins),
        out_specs=vmem,
        compiler_params=pltpu.CompilerParams(vmem_limit_bytes=16 * 1024 * 1024),
        name="diagonal",
    )(*[pltpu.with_memory_space_constraint(x, pltpu.VMEM) for x in ins])


def shifted(blocks, route, first=1):
    return [perm(block, route(i)) for i, block in enumerate(blocks, start=first)]


def gathered(own):
    mine = [own] + shifted([own] * (NX - 1), along_x)
    stack = stacked(mine)
    return mine + [perm(stack, partner)]


def local(panel, diag_tiles, dinv, u_fac, v_fac, ranks, sketch):
    panel, dinv = panel[0], dinv[0]
    u, v, ranks = u_fac[0, :, 0], v_fac[0, :, 0], ranks[0, :, 0]
    small = sketch.shape[1:]
    split = [((NX,) + small, BF16), ((NX,) + small, F32)]

    send, keep = sketch_call(ranks, v, u, sketch[0])
    got = perm(send, partner)
    panel_send, panel_keep = split_panel(panel)
    panel_got = perm(panel_send, partner)
    own, *others = pair_sum(keep, got)
    others = shifted(others, along_x)
    panel_bundles = bundles(panel_keep, panel_got, 1)
    rows = [panel_keep, panel_got] + shifted(panel_bundles, along_x)
    own_sum = owner_total(own, others)
    sums = gathered(own_sum)
    inverse = gram_inverse(own_sum)
    send, keep = sum_product(split, ranks, u, v, sums)
    got = perm(send, partner)
    own, *others = pair_sum(keep, got)
    others = shifted(others, along_x)
    tile = tile_call(own_sum, inverse, [own, *others], dinv, rows)
    cross, *blocks = tile
    arrived = shifted(blocks, to_column, 0)
    crosses = gathered(cross)
    send, keep = arrived_sum(arrived)
    got = perm(send, partner)
    here, onward = plane_sum(keep, got)
    onward = [perm(onward, along_z(1))]
    total, *mirrored = collect(here, onward)
    mirrored = shifted(mirrored, lambda d: along_upd(-d))
    panel_out = rows_call(panel, dinv, sums, crosses)
    diag_out = diag_call(diag_tiles[0], total, mirrored)
    return (panel_out[None], diag_out[None])


def solution(mesh):
    in_specs = (
        P("col", None, "upd", None),
        P("col", "upd", None),
        P("col", None, None),
        P("col", None, "upd", None, None),
        P("col", None, "upd", None, None),
        P("col", None, "upd"),
        P("col", None, None),
    )
    out_specs = (P("col", None, "upd", None), P("col", "upd", None))
    return jax.shard_map(local, mesh=mesh, in_specs=in_specs, out_specs=out_specs, check_vma=False)
```

```python
import jax
import jax.numpy as jnp
from jax import lax
from jax.experimental import pallas as pl
from jax.experimental.pallas import tpu as pltpu
from jax.sharding import PartitionSpec as P


F32 = jnp.float32
BF16 = jnp.bfloat16
AXES = ("upd", "col")
NU = 8
NX = 4
NY = 4
NZ = 8
NC = 32
HALF = 5
BLK = 128
NEAR = ((1,), (1,))
LEFT = ((0,), (0,))
EXACT = lax.Precision.HIGHEST


def dot(a, b, dims, precision=None):
    return lax.dot_general(a, b, (dims, ((), ())), precision=precision, preferred_element_type=F32)


def place():
    at = lax.axis_index("upd")
    return at >> 1, at & 1


def perm(block, route):
    pairs = []
    for u in range(NU):
        for c in range(NC):
            to = route(u, c)
            if to is not None:
                pairs.append((u * NC + c, to[0] * NC + to[1]))
    return lax.ppermute(block, AXES, pairs)


def along_x(k):
    return lambda u, c: ((u + 2 * k) % NU, c)


def along_upd(k):
    return lambda u, c: ((u + k) % NU, c)


def partner(u, c):
    return (u ^ 1, c)


def to_column(k):
    def route(u, c):
        plane, y = c // NY, c % NY
        return ((u + 2 * k) % NU, (plane + u % 2) % NZ * NY + (y + u // 2 + 1) % NY)

    return route


def along_z(k):
    return lambda u, c: (u, (c + NY * k) % NC)


def call(kernel, outs, ins, scalars=(), scratch=(), in_hbm=False):
    vmem = pl.BlockSpec(memory_space=pltpu.VMEM)
    if in_hbm:
        shapes = [jax.ShapeDtypeStruct(*out) for out in outs]
    else:
        shapes = [pltpu.VMEM(*out) for out in outs]
    out_spec = pl.BlockSpec(memory_space=pl.ANY) if in_hbm else vmem
    return pl.pallas_call(
        kernel,
        out_shape=shapes,
        in_specs=[pl.BlockSpec(memory_space=pltpu.SMEM)] * len(scalars) + [vmem] * len(ins),
        out_specs=[out_spec] * len(outs),
        scratch_shapes=list(scratch),
        compiler_params=pltpu.CompilerParams(vmem_limit_bytes=16 * 1024 * 1024),
    )(*scalars, *[pltpu.with_memory_space_constraint(x, pltpu.VMEM) for x in ins])


def masked(probe, rank):
    slots = lax.broadcasted_iota(jnp.int32, probe.shape, 0)
    return jnp.where(slots < rank, probe, 0.0).astype(BF16)


def sketch_kernel(ranks_hbm, v_hbm, u_hbm, sketch_hbm, send_ref, keep_ref, ranks, v_ref, u_ref, sketch_ref, sems):
    x, core = place()
    few = pltpu.make_async_copy(ranks_hbm, ranks, sems.at[2 * NU + 1])
    few.start()
    order = [(k, other) for k in range(NX) for other in (1, 0)]
    tiles = [((x + k) & 3) + 4 * (core ^ other) for k, other in order]
    first = pltpu.make_async_copy(sketch_hbm, sketch_ref, sems.at[2 * NU])
    first.start()
    copies = []
    for i, tile in enumerate(tiles):
        pair = (
            pltpu.make_async_copy(v_hbm.at[tile], v_ref.at[i], sems.at[2 * i]),
            pltpu.make_async_copy(u_hbm.at[tile], u_ref.at[i], sems.at[2 * i + 1]),
        )
        for copy in pair:
            copy.start()
        copies.append(pair)
    first.wait()
    few.wait()
    for i, (k, other) in enumerate(order):
        copies[i][0].wait()
        probe = masked(dot(v_ref[i], sketch_ref[...], NEAR), ranks[tiles[i]])
        copies[i][1].wait()
        out = dot(probe, u_ref[i], LEFT)
        if other:
            send_ref[k] = out.astype(BF16)
        else:
            keep_ref[k] = out


def sketch_call(ranks, v, u, sketch):
    vmem = pl.BlockSpec(memory_space=pltpu.VMEM)
    hbm = pl.BlockSpec(memory_space=pltpu.HBM)
    out = (NX,) + sketch.shape
    return pl.pallas_call(
        sketch_kernel,
        out_shape=[pltpu.VMEM(out, BF16), pltpu.VMEM(out, F32)],
        in_specs=[hbm] * 4,
        out_specs=[vmem] * 2,
        scratch_shapes=[
            pltpu.SMEM(ranks.shape, jnp.int32),
            pltpu.VMEM(v.shape, BF16),
            pltpu.VMEM(u.shape, BF16),
            pltpu.VMEM(sketch.shape, BF16),
            pltpu.SemaphoreType.DMA((2 * NU + 2,)),
        ],
        compiler_params=pltpu.CompilerParams(vmem_limit_bytes=16 * 1024 * 1024),
        name="sketch_product",
    )(*[pltpu.with_memory_space_constraint(x, pltpu.HBM) for x in (ranks, v, u, sketch)])


def project_kernel(ranks, u_ref, v_ref, *refs):
    bases, (send_ref, keep_ref) = refs[: NX + 1], refs[NX + 1 :]
    x, core = place()
    for d in range(NX):
        for other in range(2):
            tile = ((x - d) & 3) + 4 * (core ^ other)
            basis = from_source(bases, d, other)[...]
            coeff = masked(dot(u_ref[tile], basis, NEAR), ranks[tile])
            out = dot(coeff, v_ref[tile], LEFT)
            if other:
                send_ref[-d % NX] = out.astype(BF16)
            else:
                keep_ref[-d % NX] = out


def stack_kernel(a_ref, b_ref, c_ref, d_ref, out_ref):
    for k, ref in enumerate((a_ref, b_ref, c_ref, d_ref)):
        out_ref[k] = ref[...]


def stacked(blocks):
    return call(stack_kernel, [((NX,) + blocks[0].shape, BF16)], blocks)[0]


def from_source(refs, d, other):
    return refs[NX].at[d] if other else refs[d]


def sum_product(split, ranks, u, v, sums):
    return call(project_kernel, split, [u, v, *sums], [ranks])


def pair_sum_kernel(keep_ref, got_ref, own_ref, a_ref, b_ref, c_ref):
    for k, ref in enumerate((own_ref, a_ref, b_ref, c_ref)):
        ref[...] = (keep_ref[k] + got_ref[k].astype(F32)).astype(ref.dtype)


def pair_sum(keep, got):
    shape = keep.shape[1:]
    outs = [(shape, F32)] + [(shape, BF16)] * (NX - 1)
    return call(pair_sum_kernel, outs, [keep, got])


def owner_sum(own_ref, *others):
    total = own_ref[...]
    for ref in others:
        total = total + ref[...].astype(F32)
    return total


def summed_kernel(own_ref, a_ref, b_ref, c_ref, summed_ref):
    summed_ref[...] = owner_sum(own_ref, a_ref, b_ref, c_ref).astype(BF16)


def owner_total(own, others):
    return call(summed_kernel, [(own.shape, BF16)], [own, *others])[0]


def inverse_kernel(summed_ref, inverse_ref):
    summed = summed_ref[...].astype(F32)
    rk = summed.shape[0]
    gram = dot(summed, summed, NEAR, EXACT)
    rows = lax.broadcasted_iota(jnp.int32, (rk, rk), 0)
    cols = lax.broadcasted_iota(jnp.int32, (rk, rk), 1)
    row_at = lax.broadcasted_iota(jnp.int32, (rk, 1), 0)
    work = jnp.concatenate([gram, jnp.where(rows == cols, 1.0, 0.0)], axis=1)
    for k in range(rk):
        row = work[k : k + 1, :]
        scaled = row * (1.0 / work[k : k + 1, k : k + 1])
        col = jnp.where(row_at > k, work[:, k : k + 1], 0.0)
        work = work - col * scaled
    pivots = jnp.sum(jnp.where(rows == cols, work[:, :rk], 0.0), axis=1, keepdims=True)
    half = work[:, rk:] * lax.rsqrt(pivots)
    inverse_ref[...] = dot(half, half, LEFT, EXACT)


def gram_inverse(summed):
    rk = summed.shape[0]
    return call(inverse_kernel, [((rk, rk), F32)], [summed])[0]


def split_kernel(panel_ref, send_ref, keep_ref):
    x, core = place()
    for k in range(NX):
        tile = (x + k) & 3
        send_ref[k] = panel_ref[tile + 4 * (core ^ 1)]
        keep_ref[k] = panel_ref[tile + 4 * core]


def bundle_kernel(keep_ref, got_ref, *outs):
    for k, ref in enumerate(outs):
        ref[0] = keep_ref[NX - len(outs) + k]
        ref[1] = got_ref[NX - len(outs) + k]


def bundles(keep, got, first):
    shape = ((2,) + keep.shape[1:], BF16)
    return call(bundle_kernel, [shape] * (NX - first), [keep, got])


def split_panel(panel):
    shape = ((NX,) + panel.shape[1:], BF16)
    return call(split_kernel, [shape] * 2, [panel])


def tile_kernel(sum_ref, inverse_ref, own_ref, a_ref, b_ref, c_ref, dinv_ref, *refs):
    bundles, cross_ref, outs = refs[:5], refs[5], refs[6 : 6 + NX]
    updated, solved = refs[6 + NX :]
    x, core = place()
    raw = owner_sum(own_ref, a_ref, b_ref, c_ref)
    cross_ref[...] = dot(inverse_ref[...], raw, ((1,), (0,)), EXACT).astype(BF16)
    wrap = (HALF - 1) * BLK
    for d in range(NX):
        pair = ((x - d) & 3) * (2 * BLK)
        for other in range(2):
            part = (core ^ other) * BLK
            at = pl.multiple_of(pair + part, BLK)
            rows = bundles[d + 1][other] if d else bundles[other][0]
            lowrank = dot(sum_ref[:, pl.ds(at, BLK)], cross_ref[...], LEFT)
            row_block = (rows.astype(F32) - lowrank).astype(BF16)
            updated[d, pl.ds(pl.multiple_of(part, BLK), BLK)] = row_block
        result = dot(updated[d], dinv_ref[...], NEAR).astype(BF16)
        solved[pl.ds(pl.multiple_of(pair + wrap, 2 * BLK), 2 * BLK)] = result
    solved[:wrap] = solved[-wrap:]
    for k in range(NX):
        at = pl.multiple_of(((x + k) & 3) * (2 * BLK), 2 * BLK)
        product = dot(solved[pl.ds(at + wrap, 2 * BLK)], solved[pl.ds(at, (HALF + 1) * BLK)], NEAR)
        outs[k][0] = product[:BLK, : HALF * BLK].astype(BF16)
        outs[k][1] = product[BLK:, BLK:].astype(BF16)


def tile_call(summed, inverse, parts, dinv, rows):
    width = dinv.shape[0]
    out = ((2, BLK, HALF * BLK), BF16)
    return call(
        tile_kernel,
        [(summed.shape, BF16)] + [out] * NX,
        [summed, inverse, *parts, dinv, *rows],
        scratch=[
            pltpu.VMEM((NX, 2 * BLK, width), BF16),
            pltpu.VMEM((width + (HALF - 1) * BLK, width), BF16),
        ],
    )


def rows_kernel(panel_ref, dinv_ref, *refs):
    bases, crosses = refs[: NX + 1], refs[NX + 1 : 2 * NX + 2]
    out_ref, updated, solved, sems = refs[2 * NX + 2 :]
    x, core = place()
    at = pl.multiple_of((2 * x + core) * BLK, BLK)
    copies = []
    for d in range(NX):
        for other in range(2):
            tile = ((x - d) & 3) + 4 * (core ^ other)
            part = from_source(bases, d, other)[:, pl.ds(at, BLK)]
            lowrank = dot(part, from_source(crosses, d, other)[...], LEFT)
            rows = (panel_ref[tile].astype(F32) - lowrank).astype(BF16)
            updated[other * BLK : (other + 1) * BLK] = rows
        result = dot(updated[...], dinv_ref[...], NEAR).astype(BF16)
        for other in range(2):
            tile = ((x - d) & 3) + 4 * (core ^ other)
            slot = 2 * d + other
            solved[slot] = result[other * BLK : (other + 1) * BLK]
            copy = pltpu.make_async_copy(solved.at[slot], out_ref.at[tile], sems.at[slot])
            copy.start()
            copies.append(copy)
    for copy in copies:
        copy.wait()


def rows_call(panel, dinv, bases, crosses):
    return call(
        rows_kernel,
        [(panel.shape, BF16)],
        [panel, dinv, *bases, *crosses],
        scratch=[
            pltpu.VMEM((2 * BLK, panel.shape[2]), BF16),
            pltpu.VMEM(panel.shape, BF16),
            pltpu.SemaphoreType.DMA((NU,)),
        ],
        in_hbm=True,
    )[0]


def arrived_kernel(a_ref, b_ref, c_ref, d_ref, send_ref, keep_ref):
    x, core = place()
    col = lax.axis_index("col")
    y, z = col & 3, col >> 2
    valid = (core == 0) | (z > 0)
    for other in range(2):
        here, onward = 0.0, 0.0
        for k, ref in enumerate((a_ref, b_ref, c_ref, d_ref)):
            block = jnp.where(valid, ref[core ^ other].astype(F32), 0.0)
            stays = y > ((x - k) & 3)
            here = here + jnp.where(stays, block, 0.0)
            onward = onward + jnp.where(stays, 0.0, block)
        if other:
            send_ref[0] = here.astype(BF16)
            send_ref[1] = onward.astype(BF16)
        else:
            keep_ref[0] = here
            keep_ref[1] = onward


def arrived_sum(arrived):
    shape = arrived[0].shape
    return call(arrived_kernel, [(shape, BF16), (shape, F32)], arrived)


def plane_kernel(keep_ref, got_ref, here_ref, onward_ref):
    here_ref[...] = keep_ref[0] + got_ref[0].astype(F32)
    onward_ref[...] = (keep_ref[1] + got_ref[1].astype(F32)).astype(BF16)


def plane_sum(keep, got):
    shape = keep.shape[1:]
    return call(plane_kernel, [(shape, F32), (shape, BF16)], [keep, got])


def collect_kernel(here_ref, onward_ref, total_ref, a_ref, b_ref, c_ref):
    z = lax.axis_index("col") >> 2
    total = here_ref[...] + jnp.where(z > 0, onward_ref[...].astype(F32), 0.0)
    total_ref[...] = total
    for d, ref in ((1, a_ref), (2, b_ref), (3, c_ref)):
        i = HALF - 1 - d
        ref[...] = total[:, i * BLK : (i + 1) * BLK].T.astype(BF16)


def collect(here, onward):
    outs = [(here.shape, F32)] + [((BLK, BLK), BF16)] * (HALF - 2)
    return call(collect_kernel, outs, [here, *onward])


def diag_kernel(diag_ref, total_ref, a_ref, b_ref, c_ref, out_ref):
    x, core = place()
    u = 2 * x + core
    for i in range(HALF):
        at = pl.ds(pl.multiple_of(((u + i + 4) & 7) * BLK, BLK), BLK)
        out_ref[:, at] = diag_ref[:, at].astype(F32) - total_ref[:, i * BLK : (i + 1) * BLK]
    for d, ref in ((1, a_ref), (2, b_ref), (3, c_ref)):
        at = pl.ds(pl.multiple_of(((u + d) & 7) * BLK, BLK), BLK)
        out_ref[:, at] = diag_ref[:, at].astype(F32) - ref[...].astype(F32)


def diag_call(diag, total, mirrored):
    vmem = pl.BlockSpec(memory_space=pltpu.VMEM)
    ins = [diag, total, *mirrored]
    return pl.pallas_call(
        diag_kernel,
        out_shape=jax.ShapeDtypeStruct(diag.shape, F32),
        in_specs=[vmem] * len(ins),
        out_specs=vmem,
        compiler_params=pltpu.CompilerParams(vmem_limit_bytes=16 * 1024 * 1024),
        name="diagonal",
    )(*[pltpu.with_memory_space_constraint(x, pltpu.VMEM) for x in ins])


def shifted(blocks, route, first=1):
    return [perm(block, route(i)) for i, block in enumerate(blocks, start=first)]


def gathered(own):
    mine = [own] + shifted([own] * (NX - 1), along_x)
    stack = stacked(mine)
    return mine + [perm(stack, partner)]


def local(panel, diag_tiles, dinv, u_fac, v_fac, ranks, sketch):
    panel, dinv = panel[0], dinv[0]
    u, v, ranks = u_fac[0, :, 0], v_fac[0, :, 0], ranks[0, :, 0]
    small = sketch.shape[1:]
    split = [((NX,) + small, BF16), ((NX,) + small, F32)]

    send, keep = sketch_call(ranks, v, u, sketch[0])
    got = perm(send, partner)
    panel_send, panel_keep = split_panel(panel)
    panel_got = perm(panel_send, partner)
    own, *others = pair_sum(keep, got)
    others = shifted(others, along_x)
    panel_bundles = bundles(panel_keep, panel_got, 1)
    rows = [panel_keep, panel_got] + shifted(panel_bundles, along_x)
    own_sum = owner_total(own, others)
    sums = gathered(own_sum)
    inverse = gram_inverse(own_sum)
    send, keep = sum_product(split, ranks, u, v, sums)
    got = perm(send, partner)
    own, *others = pair_sum(keep, got)
    others = shifted(others, along_x)
    tile = tile_call(own_sum, inverse, [own, *others], dinv, rows)
    cross, *blocks = tile
    arrived = shifted(blocks, to_column, 0)
    crosses = gathered(cross)
    send, keep = arrived_sum(arrived)
    got = perm(send, partner)
    here, onward = plane_sum(keep, got)
    onward = [perm(onward, along_z(1))]
    total, *mirrored = collect(here, onward)
    mirrored = shifted(mirrored, lambda d: along_upd(-d))
    panel_out = rows_call(panel, dinv, sums, crosses)
    diag_out = diag_call(diag_tiles[0], total, mirrored)
    return (panel_out[None], diag_out[None])


def solution(mesh):
    in_specs = (
        P("col", None, "upd", None),
        P("col", "upd", None),
        P("col", None, None),
        P("col", None, "upd", None, None),
        P("col", None, "upd", None, None),
        P("col", None, "upd"),
        P("col", None, None),
    )
    out_specs = (P("col", None, "upd", None), P("col", "upd", None))
    return jax.shard_map(local, mesh=mesh, in_specs=in_specs, out_specs=out_specs, check_vma=False)
```

```python
import jax
import jax.numpy as jnp
from jax import lax
from jax.experimental import pallas as pl
from jax.experimental.pallas import tpu as pltpu
from jax.sharding import PartitionSpec as P


F32 = jnp.float32
BF16 = jnp.bfloat16
AXES = ("upd", "col")
NU = 8
NX = 4
NY = 4
NZ = 8
NC = 32
HALF = 5
BLK = 128
NEAR = ((1,), (1,))
LEFT = ((0,), (0,))
EXACT = lax.Precision.HIGHEST


def dot(a, b, dims, precision=None):
    return lax.dot_general(a, b, (dims, ((), ())), precision=precision, preferred_element_type=F32)


def place():
    at = lax.axis_index("upd")
    return at >> 1, at & 1


def perm(block, route):
    pairs = []
    for u in range(NU):
        for c in range(NC):
            to = route(u, c)
            if to is not None:
                pairs.append((u * NC + c, to[0] * NC + to[1]))
    return lax.ppermute(block, AXES, pairs)


def along_x(k):
    return lambda u, c: ((u + 2 * k) % NU, c)


def along_upd(k):
    return lambda u, c: ((u + k) % NU, c)


def partner(u, c):
    return (u ^ 1, c)


def to_column(k):
    def route(u, c):
        plane, y = c // NY, c % NY
        return ((u + 2 * k) % NU, (plane + u % 2) % NZ * NY + (y + u // 2 + 1) % NY)

    return route


def along_z(k):
    return lambda u, c: (u, (c + NY * k) % NC)


def call(kernel, outs, ins, scalars=(), scratch=(), in_hbm=False):
    vmem = pl.BlockSpec(memory_space=pltpu.VMEM)
    if in_hbm:
        shapes = [jax.ShapeDtypeStruct(*out) for out in outs]
    else:
        shapes = [pltpu.VMEM(*out) for out in outs]
    out_spec = pl.BlockSpec(memory_space=pl.ANY) if in_hbm else vmem
    return pl.pallas_call(
        kernel,
        out_shape=shapes,
        in_specs=[pl.BlockSpec(memory_space=pltpu.SMEM)] * len(scalars) + [vmem] * len(ins),
        out_specs=[out_spec] * len(outs),
        scratch_shapes=list(scratch),
        compiler_params=pltpu.CompilerParams(vmem_limit_bytes=16 * 1024 * 1024),
    )(*scalars, *[pltpu.with_memory_space_constraint(x, pltpu.VMEM) for x in ins])


def masked(probe, rank):
    slots = lax.broadcasted_iota(jnp.int32, probe.shape, 0)
    return jnp.where(slots < rank, probe, 0.0).astype(BF16)


def sketch_kernel(ranks_hbm, v_hbm, u_hbm, sketch_hbm, send_ref, keep_ref, ranks, v_ref, u_ref, sketch_ref, sems):
    x, core = place()
    few = pltpu.make_async_copy(ranks_hbm, ranks, sems.at[2 * NU + 1])
    few.start()
    order = [(k, other) for k in range(NX) for other in (1, 0)]
    tiles = [((x + k) & 3) + 4 * (core ^ other) for k, other in order]
    first = pltpu.make_async_copy(sketch_hbm, sketch_ref, sems.at[2 * NU])
    first.start()
    copies = []
    for i, tile in enumerate(tiles):
        pair = (
            pltpu.make_async_copy(v_hbm.at[tile], v_ref.at[i], sems.at[2 * i]),
            pltpu.make_async_copy(u_hbm.at[tile], u_ref.at[i], sems.at[2 * i + 1]),
        )
        for copy in pair:
            copy.start()
        copies.append(pair)
    first.wait()
    few.wait()
    for i, (k, other) in enumerate(order):
        copies[i][0].wait()
        probe = masked(dot(v_ref[i], sketch_ref[...], NEAR), ranks[tiles[i]])
        copies[i][1].wait()
        out = dot(probe, u_ref[i], LEFT)
        if other:
            send_ref[k] = out.astype(BF16)
        else:
            keep_ref[k] = out


def sketch_call(ranks, v, u, sketch):
    vmem = pl.BlockSpec(memory_space=pltpu.VMEM)
    hbm = pl.BlockSpec(memory_space=pltpu.HBM)
    out = (NX,) + sketch.shape
    return pl.pallas_call(
        sketch_kernel,
        out_shape=[pltpu.VMEM(out, BF16), pltpu.VMEM(out, F32)],
        in_specs=[hbm] * 4,
        out_specs=[vmem] * 2,
        scratch_shapes=[
            pltpu.SMEM(ranks.shape, jnp.int32),
            pltpu.VMEM(v.shape, BF16),
            pltpu.VMEM(u.shape, BF16),
            pltpu.VMEM(sketch.shape, BF16),
            pltpu.SemaphoreType.DMA((2 * NU + 2,)),
        ],
        compiler_params=pltpu.CompilerParams(vmem_limit_bytes=16 * 1024 * 1024),
    )(*[pltpu.with_memory_space_constraint(x, pltpu.HBM) for x in (ranks, v, u, sketch)])


def project_kernel(ranks, u_ref, v_ref, *refs):
    bases, (send_ref, keep_ref) = refs[: NX + 1], refs[NX + 1 :]
    x, core = place()
    for d in range(NX):
        for other in range(2):
            tile = ((x - d) & 3) + 4 * (core ^ other)
            basis = from_source(bases, d, other)[...]
            coeff = masked(dot(u_ref[tile], basis, NEAR), ranks[tile])
            out = dot(coeff, v_ref[tile], LEFT)
            if other:
                send_ref[-d % NX] = out.astype(BF16)
            else:
                keep_ref[-d % NX] = out


def stack_kernel(a_ref, b_ref, c_ref, d_ref, out_ref):
    for k, ref in enumerate((a_ref, b_ref, c_ref, d_ref)):
        out_ref[k] = ref[...]


def stacked(blocks):
    return call(stack_kernel, [((NX,) + blocks[0].shape, BF16)], blocks)[0]


def from_source(refs, d, other):
    return refs[NX].at[d] if other else refs[d]


def sum_product(split, ranks, u, v, sums):
    return call(project_kernel, split, [u, v, *sums], [ranks])


def pair_sum_kernel(keep_ref, got_ref, own_ref, a_ref, b_ref, c_ref):
    for k, ref in enumerate((own_ref, a_ref, b_ref, c_ref)):
        ref[...] = (keep_ref[k] + got_ref[k].astype(F32)).astype(ref.dtype)


def pair_sum(keep, got):
    shape = keep.shape[1:]
    outs = [(shape, F32)] + [(shape, BF16)] * (NX - 1)
    return call(pair_sum_kernel, outs, [keep, got])


def owner_sum(own_ref, *others):
    total = own_ref[...]
    for ref in others:
        total = total + ref[...].astype(F32)
    return total


def summed_kernel(own_ref, a_ref, b_ref, c_ref, summed_ref):
    summed_ref[...] = owner_sum(own_ref, a_ref, b_ref, c_ref).astype(BF16)


def owner_total(own, others):
    return call(summed_kernel, [(own.shape, BF16)], [own, *others])[0]


def inverse_kernel(summed_ref, inverse_ref):
    summed = summed_ref[...].astype(F32)
    rk = summed.shape[0]
    gram = dot(summed, summed, NEAR, EXACT)
    rows = lax.broadcasted_iota(jnp.int32, (rk, rk), 0)
    cols = lax.broadcasted_iota(jnp.int32, (rk, rk), 1)
    row_at = lax.broadcasted_iota(jnp.int32, (rk, 1), 0)
    work = jnp.concatenate([gram, jnp.where(rows == cols, 1.0, 0.0)], axis=1)
    for k in range(rk):
        row = work[k : k + 1, :]
        scaled = row * (1.0 / work[k : k + 1, k : k + 1])
        col = jnp.where(row_at > k, work[:, k : k + 1], 0.0)
        work = work - col * scaled
    pivots = jnp.sum(jnp.where(rows == cols, work[:, :rk], 0.0), axis=1, keepdims=True)
    half = work[:, rk:] * lax.rsqrt(pivots)
    inverse_ref[...] = dot(half, half, LEFT, EXACT)


def gram_inverse(summed):
    rk = summed.shape[0]
    return call(inverse_kernel, [((rk, rk), F32)], [summed])[0]


def split_kernel(panel_ref, send_ref, keep_ref):
    x, core = place()
    for k in range(NX):
        tile = (x + k) & 3
        send_ref[k] = panel_ref[tile + 4 * (core ^ 1)]
        keep_ref[k] = panel_ref[tile + 4 * core]


def bundle_kernel(keep_ref, got_ref, *outs):
    for k, ref in enumerate(outs):
        ref[0] = keep_ref[NX - len(outs) + k]
        ref[1] = got_ref[NX - len(outs) + k]


def bundles(keep, got, first):
    shape = ((2,) + keep.shape[1:], BF16)
    return call(bundle_kernel, [shape] * (NX - first), [keep, got])


def split_panel(panel):
    shape = ((NX,) + panel.shape[1:], BF16)
    return call(split_kernel, [shape] * 2, [panel])


def tile_kernel(sum_ref, inverse_ref, own_ref, a_ref, b_ref, c_ref, dinv_ref, *refs):
    bundles, cross_ref, outs = refs[:5], refs[5], refs[6 : 6 + NX]
    updated, solved = refs[6 + NX :]
    x, core = place()
    raw = owner_sum(own_ref, a_ref, b_ref, c_ref)
    cross_ref[...] = dot(inverse_ref[...], raw, ((1,), (0,)), EXACT).astype(BF16)
    wrap = (HALF - 1) * BLK
    for d in range(NX):
        pair = ((x - d) & 3) * (2 * BLK)
        for other in range(2):
            part = (core ^ other) * BLK
            at = pl.multiple_of(pair + part, BLK)
            rows = bundles[d + 1][other] if d else bundles[other][0]
            lowrank = dot(sum_ref[:, pl.ds(at, BLK)], cross_ref[...], LEFT)
            row_block = (rows.astype(F32) - lowrank).astype(BF16)
            updated[d, pl.ds(pl.multiple_of(part, BLK), BLK)] = row_block
        result = dot(updated[d], dinv_ref[...], NEAR).astype(BF16)
        solved[pl.ds(pl.multiple_of(pair + wrap, 2 * BLK), 2 * BLK)] = result
    solved[:wrap] = solved[-wrap:]
    for k in range(NX):
        at = pl.multiple_of(((x + k) & 3) * (2 * BLK), 2 * BLK)
        product = dot(solved[pl.ds(at + wrap, 2 * BLK)], solved[pl.ds(at, (HALF + 1) * BLK)], NEAR)
        outs[k][0] = product[:BLK, : HALF * BLK].astype(BF16)
        outs[k][1] = product[BLK:, BLK:].astype(BF16)


def tile_call(summed, inverse, parts, dinv, rows):
    width = dinv.shape[0]
    out = ((2, BLK, HALF * BLK), BF16)
    return call(tile_kernel, [(summed.shape, BF16)] + [out] * NX,
        [summed, inverse, *parts, dinv, *rows],
        scratch=[
            pltpu.VMEM((NX, 2 * BLK, width), BF16),
            pltpu.VMEM((width + (HALF - 1) * BLK, width), BF16),
        ],
    )


def rows_kernel(panel_ref, dinv_ref, *refs):
    bases, crosses = refs[: NX + 1], refs[NX + 1 : 2 * NX + 2]
    out_ref, updated, solved, sems = refs[2 * NX + 2 :]
    x, core = place()
    at = pl.multiple_of((2 * x + core) * BLK, BLK)
    copies = []
    for d in range(NX):
        for other in range(2):
            tile = ((x - d) & 3) + 4 * (core ^ other)
            part = from_source(bases, d, other)[:, pl.ds(at, BLK)]
            lowrank = dot(part, from_source(crosses, d, other)[...], LEFT)
            rows = (panel_ref[tile].astype(F32) - lowrank).astype(BF16)
            updated[other * BLK : (other + 1) * BLK] = rows
        result = dot(updated[...], dinv_ref[...], NEAR).astype(BF16)
        for other in range(2):
            tile = ((x - d) & 3) + 4 * (core ^ other)
            slot = 2 * d + other
            solved[slot] = result[other * BLK : (other + 1) * BLK]
            copy = pltpu.make_async_copy(solved.at[slot], out_ref.at[tile], sems.at[slot])
            copy.start()
            copies.append(copy)
    for copy in copies:
        copy.wait()


def rows_call(panel, dinv, bases, crosses):
    return call(rows_kernel, [(panel.shape, BF16)],
        [panel, dinv, *bases, *crosses],
        scratch=[
            pltpu.VMEM((2 * BLK, panel.shape[2]), BF16),
            pltpu.VMEM(panel.shape, BF16),
            pltpu.SemaphoreType.DMA((NU,)),
        ],
        in_hbm=True,
    )[0]


def arrived_kernel(a_ref, b_ref, c_ref, d_ref, send_ref, keep_ref):
    x, core = place()
    col = lax.axis_index("col")
    y, z = col & 3, col >> 2
    valid = (core == 0) | (z > 0)
    for other in range(2):
        here, onward = 0.0, 0.0
        for k, ref in enumerate((a_ref, b_ref, c_ref, d_ref)):
            block = jnp.where(valid, ref[core ^ other].astype(F32), 0.0)
            stays = y > ((x - k) & 3)
            here = here + jnp.where(stays, block, 0.0)
            onward = onward + jnp.where(stays, 0.0, block)
        if other:
            send_ref[0] = here.astype(BF16)
            send_ref[1] = onward.astype(BF16)
        else:
            keep_ref[0] = here
            keep_ref[1] = onward


def arrived_sum(arrived):
    shape = arrived[0].shape
    return call(arrived_kernel, [(shape, BF16), (shape, F32)], arrived)


def plane_kernel(keep_ref, got_ref, here_ref, onward_ref):
    here_ref[...] = keep_ref[0] + got_ref[0].astype(F32)
    onward_ref[...] = (keep_ref[1] + got_ref[1].astype(F32)).astype(BF16)


def plane_sum(keep, got):
    shape = keep.shape[1:]
    return call(plane_kernel, [(shape, F32), (shape, BF16)], [keep, got])


def collect_kernel(here_ref, onward_ref, total_ref, a_ref, b_ref, c_ref):
    z = lax.axis_index("col") >> 2
    total = here_ref[...] + jnp.where(z > 0, onward_ref[...].astype(F32), 0.0)
    total_ref[...] = total
    for d, ref in ((1, a_ref), (2, b_ref), (3, c_ref)):
        i = HALF - 1 - d
        ref[...] = total[:, i * BLK : (i + 1) * BLK].T.astype(BF16)


def collect(here, onward):
    outs = [(here.shape, F32)] + [((BLK, BLK), BF16)] * (HALF - 2)
    return call(collect_kernel, outs, [here, *onward])


def diag_kernel(diag_ref, total_ref, a_ref, b_ref, c_ref, out_ref):
    x, core = place()
    u = 2 * x + core
    for i in range(HALF):
        at = pl.ds(pl.multiple_of(((u + i + 4) & 7) * BLK, BLK), BLK)
        out_ref[:, at] = diag_ref[:, at].astype(F32) - total_ref[:, i * BLK : (i + 1) * BLK]
    for d, ref in ((1, a_ref), (2, b_ref), (3, c_ref)):
        at = pl.ds(pl.multiple_of(((u + d) & 7) * BLK, BLK), BLK)
        out_ref[:, at] = diag_ref[:, at].astype(F32) - ref[...].astype(F32)


def diag_call(diag, total, mirrored):
    vmem = pl.BlockSpec(memory_space=pltpu.VMEM)
    ins = [diag, total, *mirrored]
    return pl.pallas_call(
        diag_kernel,
        out_shape=jax.ShapeDtypeStruct(diag.shape, F32),
        in_specs=[vmem] * len(ins),
        out_specs=vmem,
        compiler_params=pltpu.CompilerParams(vmem_limit_bytes=16 * 1024 * 1024),
    )(*[pltpu.with_memory_space_constraint(x, pltpu.VMEM) for x in ins])


def shifted(blocks, route, first=1):
    return [perm(block, route(i)) for i, block in enumerate(blocks, start=first)]


def gathered(own):
    mine = [own] + shifted([own] * (NX - 1), along_x)
    stack = stacked(mine)
    return mine + [perm(stack, partner)]


def local(panel, diag_tiles, dinv, u_fac, v_fac, ranks, sketch):
    panel, dinv = panel[0], dinv[0]
    u, v, ranks = u_fac[0, :, 0], v_fac[0, :, 0], ranks[0, :, 0]
    small = sketch.shape[1:]
    split = [((NX,) + small, BF16), ((NX,) + small, F32)]

    send, keep = sketch_call(ranks, v, u, sketch[0])
    got = perm(send, partner)
    panel_send, panel_keep = split_panel(panel)
    panel_got = perm(panel_send, partner)
    own, *others = pair_sum(keep, got)
    others = shifted(others, along_x)
    panel_bundles = bundles(panel_keep, panel_got, 1)
    rows = [panel_keep, panel_got] + shifted(panel_bundles, along_x)
    own_sum = owner_total(own, others)
    sums = gathered(own_sum)
    inverse = gram_inverse(own_sum)
    send, keep = sum_product(split, ranks, u, v, sums)
    got = perm(send, partner)
    own, *others = pair_sum(keep, got)
    others = shifted(others, along_x)
    tile = tile_call(own_sum, inverse, [own, *others], dinv, rows)
    cross, *blocks = tile
    arrived = shifted(blocks, to_column, 0)
    crosses = gathered(cross)
    send, keep = arrived_sum(arrived)
    got = perm(send, partner)
    here, onward = plane_sum(keep, got)
    onward = [perm(onward, along_z(1))]
    total, *mirrored = collect(here, onward)
    mirrored = shifted(mirrored, lambda d: along_upd(-d))
    panel_out = rows_call(panel, dinv, sums, crosses)
    diag_out = diag_call(diag_tiles[0], total, mirrored)
    return (panel_out[None], diag_out[None])


def solution(mesh):
    in_specs = (
        P("col", None, "upd", None),
        P("col", "upd", None),
        P("col", None, None),
        P("col", None, "upd", None, None),
        P("col", None, "upd", None, None),
        P("col", None, "upd"),
        P("col", None, None),
    )
    out_specs = (P("col", None, "upd", None), P("col", "upd", None))
    return jax.shard_map(local, mesh=mesh, in_specs=in_specs, out_specs=out_specs, check_vma=False)
```
